512 devices in a mesh: row: 32 (over y, x_hi, core), col: 16 (over x_lo, z).
Axes of the slice: x: 4 (x_hi: 2, x_lo: 2; x = x_hi * 2 + x_lo), y: 8, z: 8, core: 2. Of those that a mesh axis runs over, the one named last changes fastest.
Arguments:
- tile_blocks: bfloat16 [12288, 128, 128], P(('row', 'col')), may hold values from -0.21875 to 0.21875
- tile_rows: int32 [12288], P(('row', 'col')), may hold values from 0 to 4095, as said below
- tile_cols: int32 [12288], P(('row', 'col')), may hold values from 0 to 4095, as said below
- trial_vectors: bfloat16 [4, 524288], P(None, ('col', 'row')), may hold values from -6 to 6
- basis_old: float32 [44, 524288], P(None, ('col', 'row'))
- image_old: float32 [44, 524288], P(None, ('col', 'row'))
Outputs:
- projected: float32 [48, 48], replicated
- basis_new: float32 [48, 524288], P(None, ('col', 'row'))
- image_new: float32 [48, 524288], P(None, ('col', 'row'))
The draws below stay inside these ranges and needn't reach their ends.
Inputs may be any that keep to these rules, and one draw needn't show every extreme that they name: `tile_rows`: the 24 tiles of each device with index r on row have block rows b for which (b // 8) % 32 equals r. `tile_cols`: the 24 tiles of each device with index c on col have block columns from c * 256 to (c + 1) * 256 - 1.
All inputs are finite; a program needn't handle non-finite values.
Results may differ from the reference program's by a relative error of at most 0.0003.
Values may be sent and summed in bfloat16 or wider, within the bound.
A program may use at most 64 MiB of HBM per device.

```python
import math
import jax
import jax.numpy as jnp
from jax import lax

TILE = 128
NVEC = 4
NOLD = 44
BLK = 8
KT = 24
NB = 4096
ORDER = 524288
RB = 128
CB = 256
TILES = 12288


def basis_pair(key):
    key_scale = jax.random.fold_in(key, 31)
    key_base = jax.random.fold_in(key, 32)
    key_gain = jax.random.fold_in(key, 33)
    key_noise = jax.random.fold_in(key, 34)
    position = jnp.arange(ORDER, dtype=jnp.float32) / float(ORDER)
    spread = jax.random.uniform(key_scale, (ORDER,), jnp.float32, 0.0, math.log(10.0))
    column_scale = (1.0 + 2.0 * position) * jnp.exp(spread)
    base = jax.random.normal(key_base, (NOLD, ORDER), jnp.float32)
    noise = jax.random.normal(key_noise, (NOLD, ORDER), jnp.float32)
    gains = jnp.exp(jax.random.uniform(key_gain, (NOLD, 1), jnp.float32, -1.0, 1.0))
    basis = base * column_scale[None, :]
    image = gains * basis + 0.5 * noise * column_scale[None, :]
    return (basis, image)


def draw_basis_old(key, part):
    return basis_pair(key)[0]


def draw_image_old(key, part):
    return basis_pair(key)[1]


def draw_tile_rows(key, part):
    index = jnp.arange(TILES, dtype=jnp.int32)
    device = index // KT
    col_count = RB // BLK
    row_count = CB // BLK
    row_index = device // col_count
    offset = jax.random.randint(jax.random.fold_in(key, 11), (TILES,), 0, RB, dtype=jnp.int32)
    piece_slot = offset // BLK
    inner = offset % BLK
    return ((piece_slot * row_count + row_index) * BLK + inner).astype(jnp.int32)


def draw_tile_cols(key, part):
    index = jnp.arange(TILES, dtype=jnp.int32)
    device = index // KT
    col_count = RB // BLK
    col_index = device % col_count
    offset = jax.random.randint(jax.random.fold_in(key, 12), (TILES,), 0, CB, dtype=jnp.int32)
    return (col_index * CB + offset).astype(jnp.int32)


def shard_levels(stream_key, dims, pieces, smallest, largest):
    level, own = 1.0, jax.random.fold_in(stream_key, 6)
    for dim, blocks in pieces:
        heights = jnp.exp(jax.random.uniform(jax.random.fold_in(own, dim), (blocks,), jnp.float32, smallest / len(pieces), largest / len(pieces)))
        level = level * jnp.repeat(heights, dims[dim] // blocks).reshape([-1 if axis == dim else 1 for axis in range(len(dims))])
    return level


def gaussian(own_key, dims, deviation, most, cuts=(), held_as=jnp.bfloat16):
    array = deviation * jax.random.normal(own_key, dims, jnp.float32)
    if cuts:
        array = array * shard_levels(own_key, dims, cuts, -0.22, 0.18)
    return jnp.clip(array, -most, most).astype(held_as)


def setup_inputs(seed: int = 0) -> dict:
    streams_of = jax.random.split(jax.random.key(seed), 7)
    return {
        "tile_blocks": gaussian(streams_of[0], (TILES, TILE, TILE), (2 * TILE * KT // BLK) ** -0.5, 0.21875, ((0, 512),)),
        "tile_rows": draw_tile_rows(jax.random.fold_in(streams_of[6], 71), 0),
        "tile_cols": draw_tile_cols(jax.random.fold_in(streams_of[6], 71), 0),
        "trial_vectors": gaussian(streams_of[3], (NVEC, ORDER), 1.0, 6.0, ((1, 512),)),
        "basis_old": draw_basis_old(jax.random.fold_in(streams_of[6], 71), 0),
        "image_old": draw_image_old(jax.random.fold_in(streams_of[6], 71), 0),
    }


def reference(tile_blocks, tile_rows, tile_cols, trial_vectors, basis_old, image_old):
    highest = lax.Precision.HIGHEST
    vec_blocks = trial_vectors.astype(jnp.float32).reshape(NVEC, NB, TILE)

    def per_device(items):
        blocks, rows_here, cols_here = items
        wide_blocks = blocks.astype(jnp.float32)
        forward = jnp.einsum('ktb,tab->tka', vec_blocks[:, cols_here], wide_blocks, precision=highest)
        backward = jnp.einsum('kta,tab->tkb', vec_blocks[:, rows_here], wide_blocks, precision=highest)
        return (forward, backward)
    device_count = TILES // KT
    forward, backward = lax.map(per_device, (tile_blocks.reshape(device_count, KT, TILE, TILE), tile_rows.reshape(device_count, KT), tile_cols.reshape(device_count, KT)))
    sums = jax.ops.segment_sum(forward.reshape(TILES, NVEC, TILE), tile_rows, NB)
    sums = sums + jax.ops.segment_sum(backward.reshape(TILES, NVEC, TILE), tile_cols, NB)
    image = sums.transpose(1, 0, 2).reshape(NVEC, ORDER)
    basis_all = jnp.concatenate([basis_old, trial_vectors.astype(jnp.float32)], axis=0)
    images_all = jnp.concatenate([image_old, image], axis=0)
    correlation = jnp.dot(basis_all, basis_all.T, precision=highest) / float(ORDER)
    coupling = jnp.dot(basis_all, images_all.T, precision=highest) / float(ORDER)
    factor = jnp.linalg.cholesky(correlation)

    def solve_lower(matrix):
        return lax.linalg.triangular_solve(factor, matrix, left_side=True, lower=True)
    half_done = solve_lower(coupling)
    projected = solve_lower(half_done.T).T
    return (projected, solve_lower(basis_all), solve_lower(images_all))
```

```python
import functools

import jax
import jax.numpy as jnp
from jax import lax
from jax.experimental import pallas as pl
from jax.experimental.pallas import tpu as pltpu
from jax.sharding import PartitionSpec as P

MESH = pl.DeviceIdType.MESH
F32 = jnp.float32
BF16 = jnp.bfloat16
HIGHEST = lax.Precision.HIGHEST


def dot_nt(a, b):
    return lax.dot_general(a, b, (((1,), (1,)), ((), ())), precision=HIGHEST, preferred_element_type=F32)


def dot_nn(a, b):
    return lax.dot_general(a, b, (((1,), (0,)), ((), ())), precision=HIGHEST, preferred_element_type=F32)


def lower_inverse(a):
    n = a.shape[0]
    tiles = n // 8
    sub = lax.broadcasted_iota(jnp.int32, (8, n), 0)
    lane = lax.broadcasted_iota(jnp.int32, (8, n), 1)
    left = [a[8 * i : 8 * i + 8, :] for i in range(tiles)]
    right = [jnp.where(sub + 8 * i == lane, 1.0, 0.0).astype(F32) for i in range(tiles)]
    for j in range(n):
        at, row = j // 8, j % 8
        pivot_left = left[at][row : row + 1, :]
        pivot_right = right[at][row : row + 1, :]
        inv = 1.0 / pivot_left[:, j : j + 1]
        pivot_left = pivot_left * inv
        pivot_right = pivot_right * inv
        for i in range(at, tiles):
            ratio = left[i][:, j : j + 1]
            if i == at:
                ratio = jnp.where(sub[:, :1] > row, ratio, 0.0)
            left[i] = left[i] - ratio * pivot_left
            right[i] = right[i] - ratio * pivot_right
    out = []
    for i in range(tiles):
        diag = jnp.sum(jnp.where(sub + 8 * i == lane, left[i], 0.0), axis=1, keepdims=True)
        out.append(right[i] / jnp.sqrt(diag))
    return jnp.concatenate(out, axis=0)


def kernel(
    n_row, n_col, total_cols,
    rows_s, cols_s, tiles_h, trial_h, basis_h, image_h,
    proj_o, basis_o, image_o,
    tiles, trial, old_basis, old_image, basis, image, mix,
    x_row, x_col, prod, row_send, col_send, row_recv, col_recv,
    gram, e1, e2, e3, late, a1, a2, new_basis, new_image, proj,
    loc, sem,
):
    r = lax.axis_index("row")
    c = lax.axis_index("col")
    n_old = basis_h.shape[0]
    n_vec = trial_h.shape[0]
    n_all = n_old + n_vec
    kt = tiles.shape[0]
    n_y = n_row // 4
    y, q = r // 4, r % 4

    local = [
        pltpu.make_async_copy(trial_h, trial, loc.at[0]),
        pltpu.make_async_copy(basis_h, old_basis, loc.at[1]),
        pltpu.make_async_copy(image_h, old_image, loc.at[2]),
        pltpu.make_async_copy(tiles_h, tiles, loc.at[3]),
    ]
    for copy in local:
        copy.start()

    bar = pltpu.get_barrier_semaphore()

    @pl.loop(1, n_row)
    def _(d):
        pl.semaphore_signal(bar, 1, device_id=(lax.rem(r + d, n_row), c), device_id_type=MESH)

    @pl.loop(1, n_col)
    def _(d):
        pl.semaphore_signal(bar, 1, device_id=(r, lax.rem(c + d, n_col)), device_id_type=MESH)

    local[0].wait()
    for j in range(8):
        block = trial[:, 128 * j : 128 * (j + 1)]
        x_row[r * 8 + j] = block
        x_col[c * 8 + j] = block
    pl.semaphore_wait(bar, n_row + n_col - 2)

    def rcopy(src, dst, k, dev):
        return pltpu.make_async_remote_copy(
            src, dst, sem.at[k, 0], sem.at[k, 1], device_id=dev, device_id_type=MESH
        )

    def drain(view, k):
        w = rcopy(view, view, k, (r, c))
        w.wait_send()
        w.wait_recv()

    @pl.loop(1, n_row)
    def _(d):
        own = pl.ds(r * 8, 8)
        rcopy(x_row.at[own], x_row.at[own], 0, (lax.rem(r + d, n_row), c)).start()

    @pl.loop(1, n_col)
    def _(d):
        own = pl.ds(c * 8, 8)
        rcopy(x_col.at[own], x_col.at[own], 1, (r, lax.rem(c + d, n_col))).start()

    local[1].wait()
    local[2].wait()
    basis[0:n_old, :] = old_basis[...]
    image[0:n_old, :] = old_image[...]
    basis[n_old:n_all, :] = trial[...].astype(F32)
    image[n_old:n_all, :] = jnp.zeros((n_vec, image.shape[1]), F32)
    mix[0:n_all, :] = basis[...]
    mix[n_all : 2 * n_all, :] = image[...]
    g = dot_nt(basis[...], mix[...])
    gram[...] = jnp.zeros(gram.shape, F32)
    for i in range(n_all // 8):
        gram[i, :, 0 : 2 * n_all] = g[8 * i : 8 * i + 8, :]

    e1[y] = gram[y]

    @pl.loop(1, n_y)
    def _(d):
        to = lax.rem(y + d, n_y)
        rcopy(gram.at[to], e1.at[y], 2, (to * 4 + q, c)).start()

    local[3].wait()
    drain(x_row.at[pl.ds(0, (n_row - 1) * 8)], 0)
    drain(x_col.at[pl.ds(0, (n_col - 1) * 8)], 1)

    def row_of(t):
        b = rows_s[t]
        return b // (8 * n_row) * 8 + b % 8

    def col_of(t):
        return cols_s[t] % (8 * n_row)

    prod[...] = jnp.zeros(prod.shape, F32)

    @pl.loop(0, kt // 4)
    def _(s):
        fwd, bwd = [], []
        for u in range(4):
            t = s * 4 + u
            tile = tiles[t]
            fwd.append(
                lax.dot_general(x_row[col_of(t)], tile, (((1,), (1,)), ((), ())), preferred_element_type=F32)
            )
            bwd.append(
                lax.dot_general(x_col[row_of(t)], tile, (((1,), (0,)), ((), ())), preferred_element_type=F32)
            )
        at = pl.ds(pl.multiple_of(s * 16, 16), 16)
        prod[0, at, :] = jnp.concatenate(fwd, axis=0)
        prod[1, at, :] = jnp.concatenate(bwd, axis=0)

    lane = lax.broadcasted_iota(jnp.int32, (8, 256), 1) % 128
    row_key = jnp.full((8, 256), -1, jnp.int32)
    col_key = jnp.full((8, 256), -1, jnp.int32)
    for t in range(kt):
        mine = lane // 4 == t
        row_key = jnp.where(mine, row_of(t) * 4 + lane % 4, row_key)
        col_key = jnp.where(mine, col_of(t) * 4 + lane % 4, col_key)

    def place(key, which, pieces, out):
        p = prod[which]
        high = p.astype(BF16)
        low = (p - high.astype(F32)).astype(BF16)
        both = jnp.concatenate([high, low], axis=0)
        key = jnp.concatenate([key] * 16, axis=0)
        base = lax.broadcasted_iota(jnp.int32, (128, 256), 0)

        @pl.loop(0, pieces // 4)
        def _(s):
            pick = jnp.where(base + s * 128 == key, 1.0, 0.0).astype(BF16)
            placed = lax.dot_general(pick, both, (((1,), (0,)), ((), ())), preferred_element_type=F32)
            out[pl.ds(s * 4, 4)] = placed.reshape(4, 32, 128)

    place(col_key, 1, n_row, row_send)

    @pl.loop(1, n_row)
    def _(d):
        to = lax.rem(r + d, n_row)
        rcopy(row_send.at[to], row_recv.at[d - 1], 3, (to, c)).start()

    place(row_key, 0, n_col, col_send)

    @pl.loop(1, n_col)
    def _(d):
        to = lax.rem(c + d, n_col)
        rcopy(col_send.at[to], col_recv.at[d - 1], 4, (r, to)).start()

    drain(e1.at[pl.ds(0, n_y - 1)], 2)
    part = e1[0]
    for i in range(1, n_y):
        part = part + e1[i]
    e2[q] = part

    @pl.loop(1, 4)
    def _(d):
        rcopy(e2.at[q], e2.at[q], 5, (y * 4 + lax.rem(q + d, 4), c)).start()

    drain(e2.at[pl.ds(0, 3)], 5)
    part = e2[0]
    for i in range(1, 4):
        part = part + e2[i]
    e3[c] = part

    @pl.loop(1, n_col)
    def _(d):
        rcopy(e3.at[c], e3.at[c], 6, (r, lax.rem(c + d, n_col))).start()

    drain(e3.at[pl.ds(0, n_col - 1)], 6)
    part = e3[0]
    for i in range(1, n_col):
        part = part + e3[i]
    late[0] = part

    @pl.loop(1, n_y)
    def _(d):
        rcopy(late.at[0], late.at[1 + y], 7, (lax.rem(y + d, n_y) * 4 + q, c)).start()

    late[1 + y] = part

    drain(row_recv, 3)
    drain(col_recv, 4)
    acc = row_send[r] + col_send[c]
    for i in range(n_row - 1):
        acc = acc + row_recv[i]
    for i in range(n_col - 1):
        acc = acc + col_recv[i]
    for j in range(8):
        image[n_old:n_all, 128 * j : 128 * (j + 1)] = acc[n_vec * j : n_vec * (j + 1), :]
    fresh = image[n_all - 8 : n_all, :]
    a1[r] = jnp.zeros((8, 128), F32)
    a1[r, :, 0:n_all] = dot_nt(fresh, basis[...])

    @pl.loop(1, n_row)
    def _(d):
        rcopy(a1.at[r], a1.at[r], 8, (lax.rem(r + d, n_row), c)).start()

    drain(late.at[pl.ds(1, n_y - 1)], 7)
    scale = 1.0 / total_cols
    g = jnp.concatenate([late[1 + i] for i in range(n_all // 8)], axis=0) * scale
    inverse = lower_inverse(g[:, 0:n_all])
    old_coupling = g[:, n_all : 2 * n_all]

    drain(a1.at[pl.ds(0, n_row - 1)], 8)
    part = a1[0]
    for i in range(1, n_row):
        part = part + a1[i]
    a2[c] = part

    @pl.loop(1, n_col)
    def _(d):
        rcopy(a2.at[c], a2.at[c], 9, (r, lax.rem(c + d, n_col))).start()

    new_basis[...] = dot_nn(inverse, basis[...])
    out_basis = pltpu.make_async_copy(new_basis, basis_o, loc.at[0])
    out_basis.start()
    new_image[...] = dot_nn(inverse, image[...])
    out_image = pltpu.make_async_copy(new_image, image_o, loc.at[1])
    out_image.start()
    half = dot_nn(inverse, old_coupling)

    drain(a2.at[pl.ds(0, n_col - 1)], 9)
    part = a2[0]
    for i in range(1, n_col):
        part = part + a2[i]
    fresh = part[:, 0:n_all] * scale
    pick = lax.broadcasted_iota(jnp.int32, (8, n_all), 0) + (n_all - 8)
    spot = jnp.where(
        (pick == lax.broadcasted_iota(jnp.int32, (8, n_all), 1)) & (pick >= n_old), 1.0, 0.0
    ).astype(F32)
    fresh = lax.dot_general(fresh, spot, (((0,), (0,)), ((), ())), precision=HIGHEST, preferred_element_type=F32)
    half = half + dot_nn(inverse, fresh)
    proj[...] = dot_nt(half, inverse)
    out_proj = pltpu.make_async_copy(proj, proj_o, loc.at[2])
    out_proj.start()
    out_proj.wait()
    out_basis.wait()
    out_image.wait()


def local(tile_blocks, tile_rows, tile_cols, trial_vectors, basis_old, image_old):
    n_row = lax.axis_size("row")
    n_col = lax.axis_size("col")
    kt, ts, _ = tile_blocks.shape
    n_vec, width = trial_vectors.shape
    n_old = basis_old.shape[0]
    n_all = n_old + n_vec
    n_y = n_row // 4
    any_spec = pl.BlockSpec(memory_space=pl.ANY)
    smem = pl.BlockSpec(memory_space=pltpu.SMEM)
    v = pltpu.VMEM
    return pl.pallas_call(
        functools.partial(kernel, n_row, n_col, float(width * n_row * n_col)),
        out_shape=(
            jax.ShapeDtypeStruct((n_all, n_all), F32),
            jax.ShapeDtypeStruct((n_all, width), F32),
            jax.ShapeDtypeStruct((n_all, width), F32),
        ),
        in_specs=[smem, smem, any_spec, any_spec, any_spec, any_spec],
        out_specs=(any_spec, any_spec, any_spec),
        scratch_shapes=[
            v((kt, ts, ts), BF16),
            v((n_vec, width), BF16),
            v((n_old, width), F32),
            v((n_old, width), F32),
            v((n_all, width), F32),
            v((n_all, width), F32),
            v((2 * n_all, width), F32),
            v((8 * n_row, n_vec, ts), BF16),
            v((8 * n_col, n_vec, ts), BF16),
            v((2, 128, ts), F32),
            v((n_row, 32, ts), F32),
            v((n_col, 32, ts), F32),
            v((n_row - 1, 32, ts), F32),
            v((n_col - 1, 32, ts), F32),
            v((n_y, 8, 128), F32),
            v((n_y, 8, 128), F32),
            v((4, 8, 128), F32),
            v((n_col, 8, 128), F32),
            v((n_y + 1, 8, 128), F32),
            v((n_row, 8, 128), F32),
            v((n_col, 8, 128), F32),
            v((n_all, width), F32),
            v((n_all, width), F32),
            v((n_all, n_all), F32),
            pltpu.SemaphoreType.DMA((4,)),
            pltpu.SemaphoreType.DMA((10, 2)),
        ],
        compiler_params=pltpu.CompilerParams(
            collective_id=0, has_side_effects=True, vmem_limit_bytes=32 << 20
        ),
    )(tile_rows, tile_cols, tile_blocks, trial_vectors, basis_old, image_old)


def solution(mesh):
    in_specs = (
        P(("row", "col"), None, None),
        P(("row", "col")),
        P(("row", "col")),
        P(None, ("col", "row")),
        P(None, ("col", "row")),
        P(None, ("col", "row")),
    )
    out_specs = (P(), P(None, ("col", "row")), P(None, ("col", "row")))
    return jax.shard_map(local, mesh=mesh, in_specs=in_specs, out_specs=out_specs, check_vma=False)
```

```python
import functools

import jax
import jax.numpy as jnp
from jax import lax
from jax.experimental import pallas as pl
from jax.experimental.pallas import tpu as pltpu
from jax.sharding import PartitionSpec as P

MESH = pl.DeviceIdType.MESH
F32 = jnp.float32
BF16 = jnp.bfloat16
HIGHEST = lax.Precision.HIGHEST


def dot_nt(a, b):
    return lax.dot_general(a, b, (((1,), (1,)), ((), ())), precision=HIGHEST, preferred_element_type=F32)


def dot_nn(a, b):
    return lax.dot_general(a, b, (((1,), (0,)), ((), ())), precision=HIGHEST, preferred_element_type=F32)


def lower_inverse(a):
    n = a.shape[0]
    tiles = n // 8
    sub = lax.broadcasted_iota(jnp.int32, (8, n), 0)
    lane = lax.broadcasted_iota(jnp.int32, (8, n), 1)
    left = [a[8 * i : 8 * i + 8, :] for i in range(tiles)]
    right = [jnp.where(sub + 8 * i == lane, 1.0, 0.0).astype(F32) for i in range(tiles)]
    for j in range(n):
        at, row = j // 8, j % 8
        pivot_left = left[at][row : row + 1, :]
        pivot_right = right[at][row : row + 1, :]
        inv = 1.0 / pivot_left[:, j : j + 1]
        pivot_left = pivot_left * inv
        pivot_right = pivot_right * inv
        for i in range(at, tiles):
            ratio = left[i][:, j : j + 1]
            if i == at:
                ratio = jnp.where(sub[:, :1] > row, ratio, 0.0)
            left[i] = left[i] - ratio * pivot_left
            right[i] = right[i] - ratio * pivot_right
    out = []
    for i in range(tiles):
        diag = jnp.sum(jnp.where(sub + 8 * i == lane, left[i], 0.0), axis=1, keepdims=True)
        out.append(right[i] / jnp.sqrt(diag))
    return jnp.concatenate(out, axis=0)


def kernel(
    n_row, n_col, total_cols,
    rows_h, cols_h, tiles_h, trial_h, basis_h, image_h,
    proj_o, basis_o, image_o,
    rows_s, cols_s, tiles, trial, old_basis, old_image, basis, image, mix,
    x_row, x_col, prod, prod2, keys, row_send, col_send, row_recv, col_recv,
    gram, e1, e2, e3, late, a1, a2, new_basis, new_image, proj,
    loc, sem,
):
    r = lax.axis_index("row")
    c = lax.axis_index("col")
    n_old = basis_h.shape[0]
    n_vec = trial_h.shape[0]
    n_all = n_old + n_vec
    kt = tiles.shape[0]
    n_y = n_row // 4
    y, q = r // 4, r % 4

    local = [
        pltpu.make_async_copy(trial_h, trial, loc.at[0]),
        pltpu.make_async_copy(basis_h, old_basis, loc.at[1]),
        pltpu.make_async_copy(image_h, old_image, loc.at[2]),
        pltpu.make_async_copy(tiles_h, tiles, loc.at[3]),
        pltpu.make_async_copy(rows_h, rows_s, loc.at[4]),
        pltpu.make_async_copy(cols_h, cols_s, loc.at[5]),
    ]
    for copy in local:
        copy.start()

    bar = pltpu.get_barrier_semaphore()

    @pl.loop(1, n_row)
    def _(d):
        pl.semaphore_signal(bar, 1, device_id=(lax.rem(r + d, n_row), c), device_id_type=MESH)

    @pl.loop(1, n_col)
    def _(d):
        pl.semaphore_signal(bar, 1, device_id=(r, lax.rem(c + d, n_col)), device_id_type=MESH)

    local[0].wait()
    for j in range(8):
        block = trial[:, 128 * j : 128 * (j + 1)]
        x_row[r * 8 + j] = block
        x_col[c * 8 + j] = block
    pl.semaphore_wait(bar, n_row + n_col - 2)

    def rcopy(src, dst, k, dev):
        return pltpu.make_async_remote_copy(
            src, dst, sem.at[k, 0], sem.at[k, 1], device_id=dev, device_id_type=MESH
        )

    def drain(view, k):
        w = rcopy(view, view, k, (r, c))
        w.wait_send()
        w.wait_recv()

    def far_first(i, n):
        return lax.rem(n // 2 + (i + 1) // 2 * (1 - i % 2 * 2) + n, n)

    @pl.loop(0, n_col - 1)
    def _(i):
        own = pl.ds(c * 8, 8)
        rcopy(x_col.at[own], x_col.at[own], 1, (r, lax.rem(c + far_first(i, n_col), n_col))).start()

    @pl.loop(0, n_row - 1)
    def _(i):
        own = pl.ds(r * 8, 8)
        rcopy(x_row.at[own], x_row.at[own], 0, (lax.rem(r + far_first(i, n_row), n_row), c)).start()

    local[4].wait()
    local[5].wait()

    def row_of(t):
        b = rows_s[t]
        return b // (8 * n_row) * 8 + b % 8

    def col_of(t):
        return cols_s[t] % (8 * n_row)

    lane = lax.broadcasted_iota(jnp.int32, (8, 128), 1)
    row_key = jnp.full((8, 128), -1, jnp.int32)
    col_key = jnp.full((8, 128), -1, jnp.int32)
    for t in range(kt):
        mine = lane // 4 == t
        row_key = jnp.where(mine, row_of(t) * 4 + lane % 4, row_key)
        col_key = jnp.where(mine, col_of(t) * 4 + lane % 4, col_key)
    keys[0] = col_key
    core = r % 2
    twin = (r + 1 - 2 * core, c)
    rcopy(keys.at[0], keys.at[1], 10, twin).start()

    local[1].wait()
    local[2].wait()
    basis[0:n_old, :] = old_basis[...]
    image[0:n_old, :] = old_image[...]
    basis[n_old:n_all, :] = trial[...].astype(F32)
    image[n_old:n_all, :] = jnp.zeros((n_vec, image.shape[1]), F32)
    mix[0:n_all, :] = basis[...]
    mix[n_all : 2 * n_all, :] = image[...]
    g = dot_nt(basis[...], mix[...])
    gram[...] = jnp.zeros(gram.shape, F32)
    for i in range(n_all // 8):
        gram[i, :, 0 : 2 * n_all] = g[8 * i : 8 * i + 8, :]

    e1[y] = gram[y]

    @pl.loop(1, n_y)
    def _(d):
        to = lax.rem(y + d, n_y)
        rcopy(gram.at[to], e1.at[y], 2, (to * 4 + q, c)).start()

    local[3].wait()
    prod[...] = jnp.zeros(prod.shape, F32)

    def products(which, x, index, along):
        @pl.loop(0, kt // 4)
        def _(s):
            out = []
            for u in range(4):
                t = s * 4 + u
                out.append(
                    lax.dot_general(
                        x[index(t)], tiles[t], (((1,), (along,)), ((), ())), preferred_element_type=F32)
                )
            prod[which, pl.ds(pl.multiple_of(s * 16, 16), 16), :] = jnp.concatenate(out, axis=0)

    def split(p):
        high = p.astype(BF16)
        return high, (p - high.astype(F32)).astype(BF16)

    drain(x_col.at[pl.ds(0, (n_col - 1) * 8)], 1)
    products(1, x_col, row_of, 0)
    rcopy(prod.at[1], prod2, 11, twin).start()

    drain(x_row.at[pl.ds(0, (n_row - 1) * 8)], 0)
    products(0, x_row, col_of, 1)

    drain(keys.at[1], 10)
    drain(prod2, 11)
    both = jnp.concatenate([*split(prod[1]), *split(prod2[...])], axis=0)
    key = jnp.concatenate([jnp.concatenate([keys[0]] * 2 + [keys[1]] * 2, axis=1)] * 16, axis=0)
    at = lax.broadcasted_iota(jnp.int32, (128, 512), 0)
    at = (at // 32 * 2 + core) * 32 + at % 32

    @pl.loop(0, n_row // 8)
    def _(s):
        pick = jnp.where(at + s * 256 == key, 1.0, 0.0).astype(BF16)
        placed = lax.dot_general(pick, both, (((1,), (0,)), ((), ())), preferred_element_type=F32)
        row_send[pl.ds(s * 4, 4)] = placed.reshape(4, 32, 128)

    half = n_row // 2
    pair = r // 2

    @pl.loop(0, half - 1)
    def _(i):
        d = far_first(i, half)
        to = lax.rem(pair + d, half)
        rcopy(row_send.at[to], row_recv.at[d - 1], 3, (to * 2 + core, c)).start()

    both = jnp.concatenate(split(prod[0]), axis=0)
    key = jnp.concatenate([jnp.concatenate([row_key] * 2, axis=1)] * 16, axis=0)
    at = lax.broadcasted_iota(jnp.int32, (128, 256), 0)

    @pl.loop(0, n_col // 4)
    def _(s):
        pick = jnp.where(at + s * 128 == key, 1.0, 0.0).astype(BF16)
        placed = lax.dot_general(pick, both, (((1,), (0,)), ((), ())), preferred_element_type=F32)
        col_send[pl.ds(s * 4, 4)] = placed.reshape(4, 32, 128)

    @pl.loop(0, n_col - 1)
    def _(i):
        d = far_first(i, n_col)
        to = lax.rem(c + d, n_col)
        rcopy(col_send.at[to], col_recv.at[d - 1], 4, (r, to)).start()

    drain(e1.at[pl.ds(0, n_y - 1)], 2)
    part = e1[0]
    for i in range(1, n_y):
        part = part + e1[i]
    e2[q] = part

    @pl.loop(1, 4)
    def _(d):
        rcopy(e2.at[q], e2.at[q], 5, (y * 4 + lax.rem(q + d, 4), c)).start()

    drain(e2.at[pl.ds(0, 3)], 5)
    part = e2[0]
    for i in range(1, 4):
        part = part + e2[i]
    e3[c] = part

    @pl.loop(1, n_col)
    def _(d):
        rcopy(e3.at[c], e3.at[c], 6, (r, lax.rem(c + d, n_col))).start()

    drain(e3.at[pl.ds(0, n_col - 1)], 6)
    part = e3[0]
    for i in range(1, n_col):
        part = part + e3[i]
    late[0] = part

    @pl.loop(1, n_y)
    def _(d):
        rcopy(late.at[0], late.at[1 + y], 7, (lax.rem(y + d, n_y) * 4 + q, c)).start()

    late[1 + y] = part

    drain(row_recv, 3)
    drain(col_recv, 4)
    acc = row_send[pair] + col_send[c]
    for i in range(half - 1):
        acc = acc + row_recv[i]
    for i in range(n_col - 1):
        acc = acc + col_recv[i]
    for j in range(8):
        image[n_old:n_all, 128 * j : 128 * (j + 1)] = acc[n_vec * j : n_vec * (j + 1), :]
    fresh = image[n_all - 8 : n_all, :]
    a1[r] = jnp.zeros((8, 128), F32)
    a1[r, :, 0:n_all] = dot_nt(fresh, basis[...])

    @pl.loop(1, n_row)
    def _(d):
        rcopy(a1.at[r], a1.at[r], 8, (lax.rem(r + d, n_row), c)).start()

    drain(late.at[pl.ds(1, n_y - 1)], 7)
    scale = 1.0 / total_cols
    g = jnp.concatenate([late[1 + i] for i in range(n_all // 8)], axis=0) * scale
    inverse = lower_inverse(g[:, 0:n_all])
    old_coupling = g[:, n_all : 2 * n_all]

    drain(a1.at[pl.ds(0, n_row - 1)], 8)
    part = a1[0]
    for i in range(1, n_row):
        part = part + a1[i]
    a2[c] = part

    @pl.loop(1, n_col)
    def _(d):
        rcopy(a2.at[c], a2.at[c], 9, (r, lax.rem(c + d, n_col))).start()

    new_basis[...] = dot_nn(inverse, basis[...])
    out_basis = pltpu.make_async_copy(new_basis, basis_o, loc.at[0])
    out_basis.start()
    new_image[...] = dot_nn(inverse, image[...])
    out_image = pltpu.make_async_copy(new_image, image_o, loc.at[1])
    out_image.start()
    base = dot_nt(dot_nn(inverse, old_coupling), inverse)
    last = jnp.swapaxes(inverse[:, n_all - 8 : n_all], 0, 1)
    last = jnp.where(lax.broadcasted_iota(jnp.int32, (8, n_all), 0) >= 8 - n_vec, last, 0.0)

    drain(a2.at[pl.ds(0, n_col - 1)], 9)
    part = a2[0]
    for i in range(1, n_col):
        part = part + a2[i]
    fresh = part[:, 0:n_all] * scale
    proj[...] = base + dot_nn(dot_nt(inverse, fresh), last)
    out_proj = pltpu.make_async_copy(proj, proj_o, loc.at[2])
    out_proj.start()
    out_proj.wait()
    out_basis.wait()
    out_image.wait()


def local(tile_blocks, tile_rows, tile_cols, trial_vectors, basis_old, image_old):
    n_row = lax.axis_size("row")
    n_col = lax.axis_size("col")
    kt, ts, _ = tile_blocks.shape
    n_vec, width = trial_vectors.shape
    n_old = basis_old.shape[0]
    n_all = n_old + n_vec
    n_y = n_row // 4
    hbm = pl.BlockSpec(memory_space=pltpu.HBM)
    v = pltpu.VMEM
    return pl.pallas_call(
        functools.partial(kernel, n_row, n_col, float(width * n_row * n_col)),
        out_shape=(
            jax.ShapeDtypeStruct((n_all, n_all), F32),
            jax.ShapeDtypeStruct((n_all, width), F32),
            jax.ShapeDtypeStruct((n_all, width), F32),
        ),
        in_specs=[hbm] * 6,
        out_specs=(hbm, hbm, hbm),
        scratch_shapes=[
            pltpu.SMEM((kt,), jnp.int32),
            pltpu.SMEM((kt,), jnp.int32),
            v((kt, ts, ts), BF16),
            v((n_vec, width), BF16),
            v((n_old, width), F32),
            v((n_old, width), F32),
            v((n_all, width), F32),
            v((n_all, width), F32),
            v((2 * n_all, width), F32),
            v((8 * n_row, n_vec, ts), BF16),
            v((8 * n_col, n_vec, ts), BF16),
            v((2, 128, ts), F32),
            v((128, ts), F32),
            v((2, 8, 128), jnp.int32),
            v((n_row // 2, 32, ts), F32),
            v((n_col, 32, ts), F32),
            v((n_row // 2 - 1, 32, ts), F32),
            v((n_col - 1, 32, ts), F32),
            v((n_y, 8, 128), F32),
            v((n_y, 8, 128), F32),
            v((4, 8, 128), F32),
            v((n_col, 8, 128), F32),
            v((n_y + 1, 8, 128), F32),
            v((n_row, 8, 128), F32),
            v((n_col, 8, 128), F32),
            v((n_all, width), F32),
            v((n_all, width), F32),
            v((n_all, n_all), F32),
            pltpu.SemaphoreType.DMA((6,)),
            pltpu.SemaphoreType.DMA((12, 2)),
        ],
        compiler_params=pltpu.CompilerParams(
            collective_id=0, has_side_effects=True, vmem_limit_bytes=60 << 20
        ),
    )(tile_rows, tile_cols, tile_blocks, trial_vectors, basis_old, image_old)


def solution(mesh):
    in_specs = (
        P(("row", "col"), None, None),
        P(("row", "col")),
        P(("row", "col")),
        P(None, ("col", "row")),
        P(None, ("col", "row")),
        P(None, ("col", "row")),
    )
    out_specs = (P(), P(None, ("col", "row")), P(None, ("col", "row")))
    return jax.shard_map(local, mesh=mesh, in_specs=in_specs, out_specs=out_specs, check_vma=False)
```

```python
import functools

import jax
import jax.numpy as jnp
from jax import lax
from jax.experimental import pallas as pl
from jax.experimental.pallas import tpu as pltpu
from jax.sharding import PartitionSpec as P

MESH = pl.DeviceIdType.MESH
F32 = jnp.float32
BF16 = jnp.bfloat16
HIGHEST = lax.Precision.HIGHEST


def dot_nt(a, b):
    return lax.dot_general(a, b, (((1,), (1,)), ((), ())), precision=HIGHEST, preferred_element_type=F32)


def dot_nn(a, b):
    return lax.dot_general(a, b, (((1,), (0,)), ((), ())), precision=HIGHEST, preferred_element_type=F32)


def lower_inverse(a):
    n = a.shape[0]
    tiles = n // 8
    sub = lax.broadcasted_iota(jnp.int32, (8, n), 0)
    lane = lax.broadcasted_iota(jnp.int32, (8, n), 1)
    left = [a[8 * i : 8 * i + 8, :] for i in range(tiles)]
    right = [jnp.where(sub + 8 * i == lane, 1.0, 0.0).astype(F32) for i in range(tiles)]
    for j in range(n):
        at, row = j // 8, j % 8
        pivot_left = left[at][row : row + 1, :]
        pivot_right = right[at][row : row + 1, :]
        inv = 1.0 / pivot_left[:, j : j + 1]
        pivot_left = pivot_left * inv
        pivot_right = pivot_right * inv
        for i in range(at, tiles):
            ratio = left[i][:, j : j + 1]
            if i == at:
                ratio = jnp.where(sub[:, :1] > row, ratio, 0.0)
            left[i] = left[i] - ratio * pivot_left
            right[i] = right[i] - ratio * pivot_right
    out = []
    for i in range(tiles):
        diag = jnp.sum(jnp.where(sub + 8 * i == lane, left[i], 0.0), axis=1, keepdims=True)
        out.append(right[i] / jnp.sqrt(diag))
    return jnp.concatenate(out, axis=0)


def kernel(
    n_row, n_col, total_cols,
    rows_h, cols_h, tiles_h, trial_h, basis_h, image_h,
    proj_o, basis_o, image_o,
    rows_s, cols_s, tiles, trial, old_basis, old_image, basis, image, mix,
    x_row, x_col, prod, prod2, keys, row_send, col_send, row_recv, col_recv,
    gram, e1, e2, sums, a1, a2, new_basis, new_image, proj,
    loc, sem,
):
    r = lax.axis_index("row")
    c = lax.axis_index("col")
    n_old = basis_h.shape[0]
    n_vec = trial_h.shape[0]
    n_all = n_old + n_vec
    kt = tiles.shape[0]
    pieces = n_all // 8
    step = n_row // pieces
    piece = r // step
    owner = (r % step == 0) & (piece < pieces)

    local = [
        pltpu.make_async_copy(trial_h, trial, loc.at[0]),
        pltpu.make_async_copy(basis_h, old_basis, loc.at[1]),
        pltpu.make_async_copy(image_h, old_image, loc.at[2]),
        pltpu.make_async_copy(tiles_h, tiles, loc.at[3]),
        pltpu.make_async_copy(rows_h, rows_s, loc.at[4]),
        pltpu.make_async_copy(cols_h, cols_s, loc.at[5]),
    ]
    for copy in local:
        copy.start()

    bar = pltpu.get_barrier_semaphore()

    @pl.loop(1, n_row)
    def _(d):
        pl.semaphore_signal(bar, 1, device_id=(lax.rem(r + d, n_row), c), device_id_type=MESH)

    @pl.loop(1, n_col)
    def _(d):
        pl.semaphore_signal(bar, 1, device_id=(r, lax.rem(c + d, n_col)), device_id_type=MESH)

    local[0].wait()
    for j in range(8):
        block = trial[:, 128 * j : 128 * (j + 1)]
        x_row[r * 8 + j] = block
        x_col[c * 8 + j] = block
    pl.semaphore_wait(bar, n_row + n_col - 2)

    def rcopy(src, dst, k, dev):
        return pltpu.make_async_remote_copy(
            src, dst, sem.at[k, 0], sem.at[k, 1], device_id=dev, device_id_type=MESH
        )

    def drain(view, k):
        w = rcopy(view, view, k, (r, c))
        w.wait_send()
        w.wait_recv()

    def far_first(i, n):
        return lax.rem(n // 2 + (i + 1) // 2 * (1 - i % 2 * 2) + n, n)

    @pl.loop(0, n_col - 1)
    def _(i):
        own = pl.ds(c * 8, 8)
        rcopy(x_col.at[own], x_col.at[own], 1, (r, lax.rem(c + far_first(i, n_col), n_col))).start()

    @pl.loop(0, n_row - 1)
    def _(i):
        own = pl.ds(r * 8, 8)
        rcopy(x_row.at[own], x_row.at[own], 0, (lax.rem(r + far_first(i, n_row), n_row), c)).start()

    local[4].wait()
    local[5].wait()

    def row_of(t):
        b = rows_s[t]
        return b // (8 * n_row) * 8 + b % 8

    def col_of(t):
        return cols_s[t] % (8 * n_row)

    lane = lax.broadcasted_iota(jnp.int32, (8, 128), 1)
    row_key = jnp.full((8, 128), -1, jnp.int32)
    col_key = jnp.full((8, 128), -1, jnp.int32)
    for t in range(kt):
        mine = lane // 4 == t
        row_key = jnp.where(mine, row_of(t) * 4 + lane % 4, row_key)
        col_key = jnp.where(mine, col_of(t) * 4 + lane % 4, col_key)
    keys[0] = col_key
    core = r % 2
    twin = (r + 1 - 2 * core, c)
    rcopy(keys.at[0], keys.at[1], 10, twin).start()

    local[1].wait()
    local[2].wait()
    basis[0:n_old, :] = old_basis[...]
    image[0:n_old, :] = old_image[...]
    basis[n_old:n_all, :] = trial[...].astype(F32)
    image[n_old:n_all, :] = jnp.zeros((n_vec, image.shape[1]), F32)
    mix[0:n_all, :] = basis[...]
    mix[n_all : 2 * n_all, :] = image[...]
    g = dot_nt(basis[...], mix[...])
    gram[...] = jnp.zeros(gram.shape, F32)
    for i in range(n_all // 8):
        gram[i, :, 0 : 2 * n_all] = g[8 * i : 8 * i + 8, :]

    @pl.loop(0, pieces)
    def _(p):
        @pl.when(p * step != r)
        def _():
            rcopy(gram.at[p], e1.at[r], 2, (p * step, c)).start()

    local[3].wait()
    prod[...] = jnp.zeros(prod.shape, F32)

    def products(which, x, index, along):
        @pl.loop(0, kt // 4)
        def _(s):
            out = []
            for u in range(4):
                t = s * 4 + u
                out.append(
                    lax.dot_general(
                        x[index(t)], tiles[t], (((1,), (along,)), ((), ())), preferred_element_type=F32)
                )
            prod[which, pl.ds(pl.multiple_of(s * 16, 16), 16), :] = jnp.concatenate(out, axis=0)

    def split(p):
        high = p.astype(BF16)
        return high, (p - high.astype(F32)).astype(BF16)

    drain(x_col.at[pl.ds(0, (n_col - 1) * 8)], 1)
    products(1, x_col, row_of, 0)
    rcopy(prod.at[1], prod2, 11, twin).start()

    @pl.when(owner)
    def _():
        rcopy(e1.at[pl.ds(0, n_row - 1)], e1.at[pl.ds(0, n_row - 1)], 2, (r, c)).wait_recv()
        gone = gram.at[pl.ds(0, pieces - 1)]
        rcopy(gone, gone, 2, (r, c)).wait_send()
        e1[r] = gram[piece]
        part = e1[0]
        for i in range(1, n_row):
            part = part + e1[i]
        e2[c] = part

        @pl.loop(0, n_col - 1)
        def _(i):
            rcopy(e2.at[c], e2.at[c], 5, (r, lax.rem(c + far_first(i, n_col), n_col))).start()

    @pl.when(jnp.logical_not(owner))
    def _():
        rcopy(gram, gram, 2, (r, c)).wait_send()

    drain(x_row.at[pl.ds(0, (n_row - 1) * 8)], 0)
    products(0, x_row, col_of, 1)

    drain(keys.at[1], 10)
    drain(prod2, 11)
    both = jnp.concatenate([*split(prod[1]), *split(prod2[...])], axis=0)
    key = jnp.concatenate([jnp.concatenate([keys[0]] * 2 + [keys[1]] * 2, axis=1)] * 16, axis=0)
    at = lax.broadcasted_iota(jnp.int32, (128, 512), 0)
    at = (at // 32 * 2 + core) * 32 + at % 32

    @pl.loop(0, n_row // 8)
    def _(s):
        pick = jnp.where(at + s * 256 == key, 1.0, 0.0).astype(BF16)
        placed = lax.dot_general(pick, both, (((1,), (0,)), ((), ())), preferred_element_type=F32)
        row_send[pl.ds(s * 4, 4)] = placed.reshape(4, 32, 128)

    half = n_row // 2
    pair = r // 2

    @pl.loop(0, half - 1)
    def _(i):
        d = far_first(i, half)
        to = lax.rem(pair + d, half)
        rcopy(row_send.at[to], row_recv.at[d - 1], 3, (to * 2 + core, c)).start()

    both = jnp.concatenate(split(prod[0]), axis=0)
    key = jnp.concatenate([jnp.concatenate([row_key] * 2, axis=1)] * 16, axis=0)
    at = lax.broadcasted_iota(jnp.int32, (128, 256), 0)

    @pl.loop(0, n_col // 4)
    def _(s):
        pick = jnp.where(at + s * 128 == key, 1.0, 0.0).astype(BF16)
        placed = lax.dot_general(pick, both, (((1,), (0,)), ((), ())), preferred_element_type=F32)
        col_send[pl.ds(s * 4, 4)] = placed.reshape(4, 32, 128)

    @pl.loop(0, n_col - 1)
    def _(i):
        d = far_first(i, n_col)
        to = lax.rem(c + d, n_col)
        rcopy(col_send.at[to], col_recv.at[d - 1], 4, (r, to)).start()

    @pl.when(owner)
    def _():
        drain(e2.at[pl.ds(0, n_col - 1)], 5)
        part = e2[0]
        for i in range(1, n_col):
            part = part + e2[i]
        sums[piece] = part

        @pl.loop(0, n_row - 1)
        def _(i):
            to = lax.rem(r + far_first(i, n_row), n_row)
            rcopy(sums.at[piece], sums.at[piece], 6, (to, c)).start()

    drain(row_recv, 3)
    drain(col_recv, 4)
    acc = row_send[pair] + col_send[c]
    for i in range(half - 1):
        acc = acc + row_recv[i]
    for i in range(n_col - 1):
        acc = acc + col_recv[i]
    for j in range(8):
        image[n_old:n_all, 128 * j : 128 * (j + 1)] = acc[n_vec * j : n_vec * (j + 1), :]
    fresh = image[n_all - 8 : n_all, :]
    a1[r] = jnp.zeros((8, 128), F32)
    a1[r, :, 0:n_all] = dot_nt(fresh, basis[...])

    @pl.loop(0, n_row - 1)
    def _(i):
        rcopy(a1.at[r], a1.at[r], 8, (lax.rem(r + far_first(i, n_row), n_row), c)).start()

    @pl.when(owner)
    def _():
        came = sums.at[pl.ds(0, pieces - 1)]
        rcopy(came, came, 6, (r, c)).wait_recv()
        gone = e1.at[pl.ds(0, n_row - 1)]
        rcopy(gone, gone, 6, (r, c)).wait_send()

    @pl.when(jnp.logical_not(owner))
    def _():
        rcopy(sums, sums, 6, (r, c)).wait_recv()

    scale = 1.0 / total_cols
    g = jnp.concatenate([sums[i] for i in range(pieces)], axis=0) * scale
    inverse = lower_inverse(g[:, 0:n_all])
    old_coupling = g[:, n_all : 2 * n_all]

    drain(a1.at[pl.ds(0, n_row - 1)], 8)
    part = a1[0]
    for i in range(1, n_row):
        part = part + a1[i]
    a2[c] = part

    @pl.loop(0, n_col - 1)
    def _(i):
        rcopy(a2.at[c], a2.at[c], 9, (r, lax.rem(c + far_first(i, n_col), n_col))).start()

    new_basis[...] = dot_nn(inverse, basis[...])
    out_basis = pltpu.make_async_copy(new_basis, basis_o, loc.at[0])
    out_basis.start()
    new_image[...] = dot_nn(inverse, image[...])
    out_image = pltpu.make_async_copy(new_image, image_o, loc.at[1])
    out_image.start()
    base = dot_nt(dot_nn(inverse, old_coupling), inverse)
    last = jnp.swapaxes(inverse[:, n_all - 8 : n_all], 0, 1)
    last = jnp.where(lax.broadcasted_iota(jnp.int32, (8, n_all), 0) >= 8 - n_vec, last, 0.0)

    drain(a2.at[pl.ds(0, n_col - 1)], 9)
    part = a2[0]
    for i in range(1, n_col):
        part = part + a2[i]
    fresh = part[:, 0:n_all] * scale
    proj[...] = base + dot_nn(dot_nt(inverse, fresh), last)
    out_proj = pltpu.make_async_copy(proj, proj_o, loc.at[2])
    out_proj.start()
    out_proj.wait()
    out_basis.wait()
    out_image.wait()


def hand_out(a_in, b_in, c_in, a_out, b_out, c_out, a, b, c, sem):
    loads = [pltpu.make_async_copy(x, y, sem.at[i]) for i, (x, y) in enumerate(((a_in, a), (b_in, b), (c_in, c)))]
    stores = [pltpu.make_async_copy(x, y, sem.at[3 + i]) for i, (x, y) in enumerate(((a, a_out), (b, b_out), (c, c_out)))]
    for copy in loads:
        copy.start()
    for load, store in zip(loads, stores):
        load.wait()
        store.start()
    for copy in stores:
        copy.wait()


def local(tile_blocks, tile_rows, tile_cols, trial_vectors, basis_old, image_old):
    n_row = lax.axis_size("row")
    n_col = lax.axis_size("col")
    kt, ts, _ = tile_blocks.shape
    n_vec, width = trial_vectors.shape
    n_old = basis_old.shape[0]
    n_all = n_old + n_vec
    hbm = pl.BlockSpec(memory_space=pltpu.HBM)
    v = pltpu.VMEM
    outs = pl.pallas_call(
        functools.partial(kernel, n_row, n_col, float(width * n_row * n_col)),
        out_shape=(
            jax.ShapeDtypeStruct((n_all, n_all), F32),
            jax.ShapeDtypeStruct((n_all, width), F32),
            jax.ShapeDtypeStruct((n_all, width), F32),
        ),
        in_specs=[hbm] * 6,
        out_specs=(hbm, hbm, hbm),
        scratch_shapes=[
            pltpu.SMEM((kt,), jnp.int32),
            pltpu.SMEM((kt,), jnp.int32),
            v((kt, ts, ts), BF16),
            v((n_vec, width), BF16),
            v((n_old, width), F32),
            v((n_old, width), F32),
            v((n_all, width), F32),
            v((n_all, width), F32),
            v((2 * n_all, width), F32),
            v((8 * n_row, n_vec, ts), BF16),
            v((8 * n_col, n_vec, ts), BF16),
            v((2, 128, ts), F32),
            v((128, ts), F32),
            v((2, 8, 128), jnp.int32),
            v((n_row // 2, 32, ts), F32),
            v((n_col, 32, ts), F32),
            v((n_row // 2 - 1, 32, ts), F32),
            v((n_col - 1, 32, ts), F32),
            v((n_all // 8, 8, 128), F32),
            v((n_row, 8, 128), F32),
            v((n_col, 8, 128), F32),
            v((n_all // 8, 8, 128), F32),
            v((n_row, 8, 128), F32),
            v((n_col, 8, 128), F32),
            v((n_all, width), F32),
            v((n_all, width), F32),
            v((n_all, n_all), F32),
            pltpu.SemaphoreType.DMA((6,)),
            pltpu.SemaphoreType.DMA((12, 2)),
        ],
        compiler_params=pltpu.CompilerParams(
            collective_id=0, has_side_effects=True, vmem_limit_bytes=60 << 20
        ),
    )(tile_rows, tile_cols, tile_blocks, trial_vectors, basis_old, image_old)
    return pl.pallas_call(
        hand_out,
        out_shape=tuple(jax.ShapeDtypeStruct(o.shape, o.dtype) for o in outs),
        in_specs=[hbm] * 3,
        out_specs=(hbm,) * 3,
        scratch_shapes=[v(o.shape, o.dtype) for o in outs] + [pltpu.SemaphoreType.DMA((6,))],
        compiler_params=pltpu.CompilerParams(vmem_limit_bytes=60 << 20),
    )(*outs)


def solution(mesh):
    in_specs = (
        P(("row", "col"), None, None),
        P(("row", "col")),
        P(("row", "col")),
        P(None, ("col", "row")),
        P(None, ("col", "row")),
        P(None, ("col", "row")),
    )
    out_specs = (P(), P(None, ("col", "row")), P(None, ("col", "row")))
    return jax.shard_map(local, mesh=mesh, in_specs=in_specs, out_specs=out_specs, check_vma=False)
```

```python
import functools

import jax
import jax.numpy as jnp
from jax import lax
from jax.experimental import pallas as pl
from jax.experimental.pallas import tpu as pltpu
from jax.sharding import PartitionSpec as P

MESH = pl.DeviceIdType.MESH
F32 = jnp.float32
BF16 = jnp.bfloat16
HIGHEST = lax.Precision.HIGHEST


def dot_nt(a, b):
    return lax.dot_general(a, b, (((1,), (1,)), ((), ())), precision=HIGHEST, preferred_element_type=F32)


def dot_nn(a, b):
    return lax.dot_general(a, b, (((1,), (0,)), ((), ())), precision=HIGHEST, preferred_element_type=F32)


def lower_inverse(a):
    n = a.shape[0]
    tiles = n // 8
    sub = lax.broadcasted_iota(jnp.int32, (8, n), 0)
    lane = lax.broadcasted_iota(jnp.int32, (8, n), 1)
    left = [a[8 * i : 8 * i + 8, :] for i in range(tiles)]
    right = [jnp.where(sub + 8 * i == lane, 1.0, 0.0).astype(F32) for i in range(tiles)]
    for j in range(n):
        at, row = j // 8, j % 8
        pivot_left = left[at][row : row + 1, :]
        pivot_right = right[at][row : row + 1, :]
        inv = 1.0 / pivot_left[:, j : j + 1]
        pivot_left = pivot_left * inv
        pivot_right = pivot_right * inv
        for i in range(at, tiles):
            ratio = left[i][:, j : j + 1]
            if i == at:
                ratio = jnp.where(sub[:, :1] > row, ratio, 0.0)
            left[i] = left[i] - ratio * pivot_left
            right[i] = right[i] - ratio * pivot_right
    out = []
    for i in range(tiles):
        diag = jnp.sum(jnp.where(sub + 8 * i == lane, left[i], 0.0), axis=1, keepdims=True)
        out.append(right[i] / jnp.sqrt(diag))
    return jnp.concatenate(out, axis=0)


def kernel(
    n_row, n_col, total_cols,
    rows_h, cols_h, tiles_h, trial_h, basis_h, image_h,
    proj_o, basis_o, image_o,
    rows_s, cols_s, tiles, trial, old_basis, old_image, basis, image, mix,
    x_row, x_col, prod, prod2, keys, row_send, col_send, row_recv, col_recv,
    gram, e1, e2, sums, a1, a2, new_basis, new_image, proj,
    loc, sem, relay,
):
    r = lax.axis_index("row")
    c = lax.axis_index("col")
    n_old = basis_h.shape[0]
    n_vec = trial_h.shape[0]
    n_all = n_old + n_vec
    kt = tiles.shape[0]
    pieces = n_all // 8
    step = n_row // pieces
    piece = r // step
    owner = (r % step == 0) & (piece < pieces)

    local = [
        pltpu.make_async_copy(trial_h, trial, loc.at[0]),
        pltpu.make_async_copy(basis_h, old_basis, loc.at[1]),
        pltpu.make_async_copy(image_h, old_image, loc.at[2]),
        pltpu.make_async_copy(tiles_h, tiles, loc.at[3]),
        pltpu.make_async_copy(rows_h, rows_s, loc.at[4]),
        pltpu.make_async_copy(cols_h, cols_s, loc.at[5]),
    ]
    for copy in local:
        copy.start()

    bar = pltpu.get_barrier_semaphore()

    @pl.loop(1, n_row)
    def _(d):
        pl.semaphore_signal(bar, 1, device_id=(lax.rem(r + d, n_row), c), device_id_type=MESH)

    @pl.loop(1, n_col)
    def _(d):
        pl.semaphore_signal(bar, 1, device_id=(r, lax.rem(c + d, n_col)), device_id_type=MESH)

    local[0].wait()
    for j in range(8):
        block = trial[:, 128 * j : 128 * (j + 1)]
        x_row[r * 8 + j] = block
        x_col[c * 8 + j] = block
    pl.semaphore_wait(bar, n_row + n_col - 2)

    def rcopy(src, dst, k, dev):
        return pltpu.make_async_remote_copy(
            src, dst, sem.at[k, 0], sem.at[k, 1], device_id=dev, device_id_type=MESH
        )

    def drain(view, k):
        w = rcopy(view, view, k, (r, c))
        w.wait_send()
        w.wait_recv()

    def far_first(i, n):
        return lax.rem(n // 2 + (i + 1) // 2 * (1 - i % 2 * 2) + n, n)

    @pl.loop(0, n_col - 1)
    def _(i):
        own = pl.ds(c * 8, 8)
        rcopy(x_col.at[own], x_col.at[own], 1, (r, lax.rem(c + far_first(i, n_col), n_col))).start()

    half = n_row // 2
    pair = r // 2
    core = r % 2
    twin = (r + 1 - 2 * core, c)
    own = pl.ds(r * 8, 8)

    @pl.loop(0, half - 1)
    def _(i):
        d = far_first(i, half)
        to = lax.rem(pair + d, half) * 2 + core
        pltpu.make_async_remote_copy(
            x_row.at[own], x_row.at[own], sem.at[0, 0], relay.at[d], device_id=(to, c), device_id_type=MESH
        ).start()

    rcopy(x_row.at[own], x_row.at[own], 7, twin).start()

    local[4].wait()
    local[5].wait()

    def row_of(t):
        b = rows_s[t]
        return b // (8 * n_row) * 8 + b % 8

    def col_of(t):
        return cols_s[t] % (8 * n_row)

    lane = lax.broadcasted_iota(jnp.int32, (8, 128), 1)
    row_key = jnp.full((8, 128), -1, jnp.int32)
    col_key = jnp.full((8, 128), -1, jnp.int32)
    for t in range(kt):
        mine = lane // 4 == t
        row_key = jnp.where(mine, row_of(t) * 4 + lane % 4, row_key)
        col_key = jnp.where(mine, col_of(t) * 4 + lane % 4, col_key)
    keys[0] = col_key
    rcopy(keys.at[0], keys.at[1], 10, twin).start()

    local[1].wait()
    local[2].wait()
    basis[0:n_old, :] = old_basis[...]
    image[0:n_old, :] = old_image[...]
    basis[n_old:n_all, :] = trial[...].astype(F32)
    image[n_old:n_all, :] = jnp.zeros((n_vec, image.shape[1]), F32)
    mix[0:n_all, :] = basis[...]
    mix[n_all : 2 * n_all, :] = image[...]
    g = dot_nt(basis[...], mix[...])
    gram[...] = jnp.zeros(gram.shape, F32)
    for i in range(n_all // 8):
        gram[i, :, 0 : 2 * n_all] = g[8 * i : 8 * i + 8, :]

    @pl.loop(0, pieces)
    def _(p):
        @pl.when(p * step != r)
        def _():
            rcopy(gram.at[p], e1.at[r], 2, (p * step, c)).start()

    local[3].wait()
    prod[...] = jnp.zeros(prod.shape, F32)

    def products(which, x, index, along):
        @pl.loop(0, kt // 4)
        def _(s):
            out = []
            for u in range(4):
                t = s * 4 + u
                out.append(
                    lax.dot_general(
                        x[index(t)], tiles[t], (((1,), (along,)), ((), ())), preferred_element_type=F32)
                )
            prod[which, pl.ds(pl.multiple_of(s * 16, 16), 16), :] = jnp.concatenate(out, axis=0)

    def split(p):
        high = p.astype(BF16)
        return high, (p - high.astype(F32)).astype(BF16)

    drain(x_col.at[pl.ds(0, (n_col - 1) * 8)], 1)
    products(1, x_col, row_of, 0)
    rcopy(prod.at[1], prod2, 11, twin).start()

    @pl.when(owner)
    def _():
        rcopy(e1.at[pl.ds(0, n_row - 1)], e1.at[pl.ds(0, n_row - 1)], 2, (r, c)).wait_recv()
        gone = gram.at[pl.ds(0, pieces - 1)]
        rcopy(gone, gone, 2, (r, c)).wait_send()
        e1[r] = gram[piece]
        part = e1[0]
        for i in range(1, n_row):
            part = part + e1[i]
        e2[c] = part

        @pl.loop(0, n_col - 1)
        def _(i):
            rcopy(e2.at[c], e2.at[c], 5, (r, lax.rem(c + far_first(i, n_col), n_col))).start()

    @pl.when(jnp.logical_not(owner))
    def _():
        rcopy(gram, gram, 2, (r, c)).wait_send()

    @pl.loop(0, half - 1)
    def _(i):
        d = far_first(half - 2 - i, half)
        at = pl.ds(lax.rem(pair - d + half, half) * 16 + core * 8, 8)
        piece_in = x_row.at[at]
        pltpu.make_async_remote_copy(
            piece_in, piece_in, sem.at[0, 0], relay.at[d], device_id=(r, c), device_id_type=MESH
        ).wait_recv()
        rcopy(piece_in, piece_in, 7, twin).start()

    drain(keys.at[1], 10)
    drain(prod2, 11)
    both = jnp.concatenate([*split(prod[1]), *split(prod2[...])], axis=0)
    key = jnp.concatenate([jnp.concatenate([keys[0]] * 2 + [keys[1]] * 2, axis=1)] * 16, axis=0)
    at = lax.broadcasted_iota(jnp.int32, (128, 512), 0)
    at = (at // 32 * 2 + core) * 32 + at % 32

    @pl.loop(0, n_row // 8)
    def _(s):
        pick = jnp.where(at + s * 256 == key, 1.0, 0.0).astype(BF16)
        placed = lax.dot_general(pick, both, (((1,), (0,)), ((), ())), preferred_element_type=F32)
        row_send[pl.ds(s * 4, 4)] = placed.reshape(4, 32, 128)

    @pl.loop(0, half - 1)
    def _(i):
        d = far_first(i, half)
        to = lax.rem(pair + d, half)
        rcopy(row_send.at[to], row_recv.at[d - 1], 3, (to * 2 + core, c)).start()

    drain(x_row.at[pl.ds(0, half * 8)], 7)
    sent = x_row.at[pl.ds(0, (half - 1) * 8)]
    rcopy(sent, sent, 0, (r, c)).wait_send()
    products(0, x_row, col_of, 1)
    both = jnp.concatenate(split(prod[0]), axis=0)
    key = jnp.concatenate([jnp.concatenate([row_key] * 2, axis=1)] * 16, axis=0)
    at = lax.broadcasted_iota(jnp.int32, (128, 256), 0)

    @pl.loop(0, n_col // 4)
    def _(s):
        pick = jnp.where(at + s * 128 == key, 1.0, 0.0).astype(BF16)
        placed = lax.dot_general(pick, both, (((1,), (0,)), ((), ())), preferred_element_type=F32)
        col_send[pl.ds(s * 4, 4)] = placed.reshape(4, 32, 128)

    @pl.loop(0, n_col - 1)
    def _(i):
        d = far_first(i, n_col)
        to = lax.rem(c + d, n_col)
        rcopy(col_send.at[to], col_recv.at[d - 1], 4, (r, to)).start()

    @pl.when(owner)
    def _():
        drain(e2.at[pl.ds(0, n_col - 1)], 5)
        part = e2[0]
        for i in range(1, n_col):
            part = part + e2[i]
        sums[piece] = part

        @pl.loop(0, n_row - 1)
        def _(i):
            to = lax.rem(r + far_first(i, n_row), n_row)
            rcopy(sums.at[piece], sums.at[piece], 6, (to, c)).start()

    drain(row_recv, 3)
    drain(col_recv, 4)
    acc = row_send[pair] + col_send[c]
    for i in range(half - 1):
        acc = acc + row_recv[i]
    for i in range(n_col - 1):
        acc = acc + col_recv[i]
    for j in range(8):
        image[n_old:n_all, 128 * j : 128 * (j + 1)] = acc[n_vec * j : n_vec * (j + 1), :]
    fresh = image[n_all - 8 : n_all, :]
    fresh = dot_nt(fresh, basis[...])
    a1[r] = jnp.zeros((2, 128), F32)
    a1[r, :, 0:n_all] = fresh[4:6, :]
    a1[r, :, 64 : 64 + n_all] = fresh[6:8, :]

    @pl.loop(0, n_row - 1)
    def _(i):
        rcopy(a1.at[r], a1.at[r], 8, (lax.rem(r + far_first(i, n_row), n_row), c)).start()

    @pl.when(owner)
    def _():
        came = sums.at[pl.ds(0, pieces - 1)]
        rcopy(came, came, 6, (r, c)).wait_recv()
        gone = e1.at[pl.ds(0, n_row - 1)]
        rcopy(gone, gone, 6, (r, c)).wait_send()

    @pl.when(jnp.logical_not(owner))
    def _():
        rcopy(sums, sums, 6, (r, c)).wait_recv()

    scale = 1.0 / total_cols
    g = jnp.concatenate([sums[i] for i in range(pieces)], axis=0) * scale
    inverse = lower_inverse(g[:, 0:n_all])
    old_coupling = g[:, n_all : 2 * n_all]

    drain(a1.at[pl.ds(0, n_row - 1)], 8)
    part = a1[0]
    for i in range(1, n_row):
        part = part + a1[i]
    a2[c] = part

    @pl.loop(0, n_col - 1)
    def _(i):
        rcopy(a2.at[c], a2.at[c], 9, (r, lax.rem(c + far_first(i, n_col), n_col))).start()

    new_basis[...] = dot_nn(inverse, basis[...])
    out_basis = pltpu.make_async_copy(new_basis, basis_o, loc.at[0])
    out_basis.start()
    new_image[...] = dot_nn(inverse, image[...])
    out_image = pltpu.make_async_copy(new_image, image_o, loc.at[1])
    out_image.start()
    base = dot_nt(dot_nn(inverse, old_coupling), inverse)
    last = jnp.swapaxes(inverse[:, n_all - 8 : n_all], 0, 1)
    last = jnp.where(lax.broadcasted_iota(jnp.int32, (8, n_all), 0) >= 8 - n_vec, last, 0.0)

    drain(a2.at[pl.ds(0, n_col - 1)], 9)
    part = a2[0]
    for i in range(1, n_col):
        part = part + a2[i]
    fresh = jnp.concatenate([jnp.zeros((4, n_all), F32), part[:, 0:n_all], part[:, 64 : 64 + n_all]], axis=0) * scale
    proj[...] = base + dot_nn(dot_nt(inverse, fresh), last)
    out_proj = pltpu.make_async_copy(proj, proj_o, loc.at[2])
    out_proj.start()
    out_proj.wait()
    out_basis.wait()
    out_image.wait()


def hand_out(a_in, b_in, c_in, a_out, b_out, c_out, sem):
    copies = [
        pltpu.make_async_copy(b_in, b_out, sem.at[0]),
        pltpu.make_async_copy(c_in, c_out, sem.at[1]),
        pltpu.make_async_copy(a_in, a_out, sem.at[2]),
    ]
    for copy in copies:
        copy.start()
    for copy in copies:
        copy.wait()


def local(tile_blocks, tile_rows, tile_cols, trial_vectors, basis_old, image_old):
    n_row = lax.axis_size("row")
    n_col = lax.axis_size("col")
    kt, ts, _ = tile_blocks.shape
    n_vec, width = trial_vectors.shape
    n_old = basis_old.shape[0]
    n_all = n_old + n_vec
    hbm = pl.BlockSpec(memory_space=pltpu.HBM)
    v = pltpu.VMEM
    operands = [
        pltpu.with_memory_space_constraint(x, pltpu.HBM)
        for x in (tile_rows, tile_cols, tile_blocks, trial_vectors, basis_old, image_old)
    ]
    outs = pl.pallas_call(
        functools.partial(kernel, n_row, n_col, float(width * n_row * n_col)),
        out_shape=(
            jax.ShapeDtypeStruct((n_all, n_all), F32),
            jax.ShapeDtypeStruct((n_all, width), F32),
            jax.ShapeDtypeStruct((n_all, width), F32),
        ),
        in_specs=[hbm] * 6,
        out_specs=(pl.BlockSpec(memory_space=pl.ANY),) * 3,
        scratch_shapes=[
            pltpu.SMEM((kt,), jnp.int32),
            pltpu.SMEM((kt,), jnp.int32),
            v((kt, ts, ts), BF16),
            v((n_vec, width), BF16),
            v((n_old, width), F32),
            v((n_old, width), F32),
            v((n_all, width), F32),
            v((n_all, width), F32),
            v((2 * n_all, width), F32),
            v((8 * n_row, n_vec, ts), BF16),
            v((8 * n_col, n_vec, ts), BF16),
            v((2, 128, ts), F32),
            v((128, ts), F32),
            v((2, 8, 128), jnp.int32),
            v((n_row // 2, 32, ts), F32),
            v((n_col, 32, ts), F32),
            v((n_row // 2 - 1, 32, ts), F32),
            v((n_col - 1, 32, ts), F32),
            v((n_all // 8, 8, 128), F32),
            v((n_row, 8, 128), F32),
            v((n_col, 8, 128), F32),
            v((n_all // 8, 8, 128), F32),
            v((n_row, 2, 128), F32),
            v((n_col, 2, 128), F32),
            v((n_all, width), F32),
            v((n_all, width), F32),
            v((n_all, n_all), F32),
            pltpu.SemaphoreType.DMA((6,)),
            pltpu.SemaphoreType.DMA((12, 2)),
            pltpu.SemaphoreType.DMA((n_row // 2,)),
        ],
        compiler_params=pltpu.CompilerParams(
            collective_id=0, has_side_effects=True, vmem_limit_bytes=32 << 20
        ),
    )(*operands)
    return pl.pallas_call(
        hand_out,
        out_shape=tuple(jax.ShapeDtypeStruct(o.shape, o.dtype) for o in outs),
        in_specs=[pl.BlockSpec(memory_space=pl.ANY)] * 3,
        out_specs=(hbm,) * 3,
        scratch_shapes=[pltpu.SemaphoreType.DMA((3,))],
        compiler_params=pltpu.CompilerParams(vmem_limit_bytes=32 << 20),
    )(*outs)


def solution(mesh):
    in_specs = (
        P(("row", "col"), None, None),
        P(("row", "col")),
        P(("row", "col")),
        P(None, ("col", "row")),
        P(None, ("col", "row")),
        P(None, ("col", "row")),
    )
    out_specs = (P(), P(None, ("col", "row")), P(None, ("col", "row")))
    return jax.shard_map(local, mesh=mesh, in_specs=in_specs, out_specs=out_specs, check_vma=False)
```

```python
import functools

import jax
import jax.numpy as jnp
from jax import lax
from jax.experimental import pallas as pl
from jax.experimental.pallas import tpu as pltpu
from jax.sharding import PartitionSpec as P

MESH = pl.DeviceIdType.MESH
F32 = jnp.float32
BF16 = jnp.bfloat16
HIGHEST = lax.Precision.HIGHEST


def dot_nt(a, b):
    return lax.dot_general(a, b, (((1,), (1,)), ((), ())), precision=HIGHEST, preferred_element_type=F32)


def dot_nn(a, b):
    return lax.dot_general(a, b, (((1,), (0,)), ((), ())), precision=HIGHEST, preferred_element_type=F32)


def lower_inverse(a):
    n = a.shape[0]
    tiles = n // 8
    sub = lax.broadcasted_iota(jnp.int32, (8, n), 0)
    lane = lax.broadcasted_iota(jnp.int32, (8, n), 1)
    left = [a[8 * i : 8 * i + 8, :] for i in range(tiles)]
    right = [jnp.where(sub + 8 * i == lane, 1.0, 0.0).astype(F32) for i in range(tiles)]
    for j in range(n):
        at, row = j // 8, j % 8
        pivot_left = left[at][row : row + 1, :]
        pivot_right = right[at][row : row + 1, :]
        inv = 1.0 / pivot_left[:, j : j + 1]
        pivot_left = pivot_left * inv
        pivot_right = pivot_right * inv
        for i in range(at, tiles):
            ratio = left[i][:, j : j + 1]
            if i == at:
                ratio = jnp.where(sub[:, :1] > row, ratio, 0.0)
            left[i] = left[i] - ratio * pivot_left
            right[i] = right[i] - ratio * pivot_right
    out = []
    for i in range(tiles):
        diag = jnp.sum(jnp.where(sub + 8 * i == lane, left[i], 0.0), axis=1, keepdims=True)
        out.append(right[i] / jnp.sqrt(diag))
    return jnp.concatenate(out, axis=0)


def kernel(
    n_row, n_col, total_cols,
    rows_h, cols_h, tiles_h, trial_h, basis_h, image_h,
    proj_o, basis_o, image_o,
    rows_s, cols_s, tiles, trial, old_basis, old_image, basis, image, mix,
    x_row, x_col, prod, prod2, keys, pick_row, pick_col, row_send, col_send, row_recv, col_recv,
    gram, e1, e2, sums, a1, a2, new_basis, new_image, proj,
    loc, sem, relay,
):
    r = lax.axis_index("row")
    c = lax.axis_index("col")
    n_old = basis_h.shape[0]
    n_vec = trial_h.shape[0]
    n_all = n_old + n_vec
    kt = tiles.shape[0]
    pieces = n_all // 8
    step = n_row // pieces
    piece = r // step
    owner = (r % step == 0) & (piece < pieces)

    local = [
        pltpu.make_async_copy(trial_h, trial, loc.at[0]),
        pltpu.make_async_copy(basis_h, old_basis, loc.at[1]),
        pltpu.make_async_copy(image_h, old_image, loc.at[2]),
        pltpu.make_async_copy(tiles_h, tiles, loc.at[3]),
        pltpu.make_async_copy(rows_h, rows_s, loc.at[4]),
        pltpu.make_async_copy(cols_h, cols_s, loc.at[5]),
    ]
    for copy in local:
        copy.start()

    bar = pltpu.get_barrier_semaphore()

    @pl.loop(1, n_row)
    def _(d):
        pl.semaphore_signal(bar, 1, device_id=(lax.rem(r + d, n_row), c), device_id_type=MESH)

    @pl.loop(1, n_col)
    def _(d):
        pl.semaphore_signal(bar, 1, device_id=(r, lax.rem(c + d, n_col)), device_id_type=MESH)

    local[0].wait()
    for j in range(8):
        block = trial[:, 128 * j : 128 * (j + 1)]
        x_row[r * 8 + j] = block
        x_col[c * 8 + j] = block
    pl.semaphore_wait(bar, n_row + n_col - 2)

    def rcopy(src, dst, k, dev):
        return pltpu.make_async_remote_copy(
            src, dst, sem.at[k, 0], sem.at[k, 1], device_id=dev, device_id_type=MESH
        )

    def drain(view, k):
        w = rcopy(view, view, k, (r, c))
        w.wait_send()
        w.wait_recv()

    def far_first(i, n):
        return lax.rem(n // 2 + (i + 1) // 2 * (1 - i % 2 * 2) + n, n)

    @pl.loop(0, n_col - 1)
    def _(i):
        own = pl.ds(c * 8, 8)
        rcopy(x_col.at[own], x_col.at[own], 1, (r, lax.rem(c + far_first(i, n_col), n_col))).start()

    half = n_row // 2
    pair = r // 2
    core = r % 2
    twin = (r + 1 - 2 * core, c)
    own = pl.ds(r * 8, 8)

    @pl.loop(0, half - 1)
    def _(i):
        d = far_first(i, half)
        to = lax.rem(pair + d, half) * 2 + core
        pltpu.make_async_remote_copy(
            x_row.at[own], x_row.at[own], sem.at[0, 0], relay.at[d], device_id=(to, c), device_id_type=MESH
        ).start()

    rcopy(x_row.at[own], x_row.at[own], 7, twin).start()

    local[4].wait()
    local[5].wait()

    def row_of(t):
        b = rows_s[t]
        return b // (8 * n_row) * 8 + b % 8

    def col_of(t):
        return cols_s[t] % (8 * n_row)

    lane = lax.broadcasted_iota(jnp.int32, (8, 128), 1)
    row_key = jnp.full((8, 128), -1, jnp.int32)
    col_key = jnp.full((8, 128), -1, jnp.int32)
    for t in range(kt):
        mine = lane // 4 == t
        row_key = jnp.where(mine, row_of(t) * 4 + lane % 4, row_key)
        col_key = jnp.where(mine, col_of(t) * 4 + lane % 4, col_key)
    keys[0] = col_key
    rcopy(keys.at[0], keys.at[1], 10, twin).start()

    local[1].wait()
    local[2].wait()
    basis[0:n_old, :] = old_basis[...]
    image[0:n_old, :] = old_image[...]
    basis[n_old:n_all, :] = trial[...].astype(F32)
    image[n_old:n_all, :] = jnp.zeros((n_vec, image.shape[1]), F32)
    mix[0:n_all, :] = basis[...]
    mix[n_all : 2 * n_all, :] = image[...]
    g = dot_nt(basis[...], mix[...])
    gram[...] = jnp.zeros(gram.shape, F32)
    for i in range(n_all // 8):
        gram[i, :, 0 : 2 * n_all] = g[8 * i : 8 * i + 8, :]

    @pl.loop(0, pieces)
    def _(p):
        @pl.when(p * step != r)
        def _():
            rcopy(gram.at[p], e1.at[r], 2, (p * step, c)).start()

    drain(keys.at[1], 10)
    key = jnp.concatenate([jnp.concatenate([keys[0]] * 2 + [keys[1]] * 2, axis=1)] * 16, axis=0)
    at = lax.broadcasted_iota(jnp.int32, (128, 512), 0)
    at = (at // 32 * 2 + core) * 32 + at % 32

    @pl.loop(0, half // 4)
    def _(s):
        pick_row[s] = jnp.where(at + s * 256 == key, 1.0, 0.0).astype(BF16)

    key2 = jnp.concatenate([jnp.concatenate([row_key] * 2, axis=1)] * 16, axis=0)
    at2 = lax.broadcasted_iota(jnp.int32, (128, 256), 0)

    @pl.loop(0, n_col // 4)
    def _(s):
        pick_col[s] = jnp.where(at2 + s * 128 == key2, 1.0, 0.0).astype(BF16)

    local[3].wait()
    prod[...] = jnp.zeros(prod.shape, F32)

    def products(which, x, index, along):
        if True:
            out = []
            for t in range(kt):
                out.append(
                    lax.dot_general(
                        x[index(t)], tiles[t], (((1,), (along,)), ((), ())), preferred_element_type=F32)
                )
            prod[which, 0 : 4 * kt, :] = jnp.concatenate(out, axis=0)

    def split(p):
        high = p.astype(BF16)
        return high, (p - high.astype(F32)).astype(BF16)

    drain(x_col.at[pl.ds(0, (n_col - 1) * 8)], 1)
    products(1, x_col, row_of, 0)
    rcopy(prod.at[1], prod2, 11, twin).start()

    @pl.when(owner)
    def _():
        rcopy(e1.at[pl.ds(0, n_row - 1)], e1.at[pl.ds(0, n_row - 1)], 2, (r, c)).wait_recv()
        gone = gram.at[pl.ds(0, pieces - 1)]
        rcopy(gone, gone, 2, (r, c)).wait_send()
        e1[r] = gram[piece]
        part = e1[0]
        for i in range(1, n_row):
            part = part + e1[i]
        e2[c] = part

        @pl.loop(0, n_col - 1)
        def _(i):
            rcopy(e2.at[c], e2.at[c], 5, (r, lax.rem(c + far_first(i, n_col), n_col))).start()

    @pl.when(jnp.logical_not(owner))
    def _():
        rcopy(gram, gram, 2, (r, c)).wait_send()

    @pl.loop(0, half - 1)
    def _(i):
        d = far_first(half - 2 - i, half)
        at = pl.ds(lax.rem(pair - d + half, half) * 16 + core * 8, 8)
        piece_in = x_row.at[at]
        pltpu.make_async_remote_copy(
            piece_in, piece_in, sem.at[0, 0], relay.at[d], device_id=(r, c), device_id_type=MESH
        ).wait_recv()
        rcopy(piece_in, piece_in, 7, twin).start()

    drain(prod2, 11)
    both = jnp.concatenate([*split(prod[1]), *split(prod2[...])], axis=0)

    for s in range(half // 4):
        placed = lax.dot_general(pick_row[s], both, (((1,), (0,)), ((), ())), preferred_element_type=F32)
        row_send[4 * s : 4 * s + 4] = placed.reshape(4, 32, 128)

    @pl.loop(0, half - 1)
    def _(i):
        d = far_first(i, half)
        to = lax.rem(pair + d, half)
        rcopy(row_send.at[to], row_recv.at[d - 1], 3, (to * 2 + core, c)).start()

    drain(x_row.at[pl.ds(0, half * 8)], 7)
    sent = x_row.at[pl.ds(0, (half - 1) * 8)]
    rcopy(sent, sent, 0, (r, c)).wait_send()
    products(0, x_row, col_of, 1)
    both = jnp.concatenate(split(prod[0]), axis=0)

    for s in range(n_col // 4):
        placed = lax.dot_general(pick_col[s], both, (((1,), (0,)), ((), ())), preferred_element_type=F32)
        col_send[4 * s : 4 * s + 4] = placed.reshape(4, 32, 128)

    @pl.loop(0, n_col - 1)
    def _(i):
        d = far_first(i, n_col)
        to = lax.rem(c + d, n_col)
        rcopy(col_send.at[to], col_recv.at[d - 1], 4, (r, to)).start()

    @pl.when(owner)
    def _():
        drain(e2.at[pl.ds(0, n_col - 1)], 5)
        part = e2[0]
        for i in range(1, n_col):
            part = part + e2[i]
        sums[piece] = part

        @pl.loop(0, n_row - 1)
        def _(i):
            to = lax.rem(r + far_first(i, n_row), n_row)
            rcopy(sums.at[piece], sums.at[piece], 6, (to, c)).start()

    drain(row_recv, 3)
    drain(col_recv, 4)
    acc = row_send[pair] + col_send[c]
    for i in range(half - 1):
        acc = acc + row_recv[i]
    for i in range(n_col - 1):
        acc = acc + col_recv[i]
    for j in range(8):
        image[n_old:n_all, 128 * j : 128 * (j + 1)] = acc[n_vec * j : n_vec * (j + 1), :]
    fresh = image[n_all - 8 : n_all, :]
    fresh = dot_nt(fresh, basis[...])
    a1[r] = jnp.zeros((2, 128), F32)
    a1[r, :, 0:n_all] = fresh[4:6, :]
    a1[r, :, 64 : 64 + n_all] = fresh[6:8, :]

    @pl.loop(0, n_row - 1)
    def _(i):
        rcopy(a1.at[r], a1.at[r], 8, (lax.rem(r + far_first(i, n_row), n_row), c)).start()

    @pl.when(owner)
    def _():
        came = sums.at[pl.ds(0, pieces - 1)]
        rcopy(came, came, 6, (r, c)).wait_recv()
        gone = e1.at[pl.ds(0, n_row - 1)]
        rcopy(gone, gone, 6, (r, c)).wait_send()

    @pl.when(jnp.logical_not(owner))
    def _():
        rcopy(sums, sums, 6, (r, c)).wait_recv()

    scale = 1.0 / total_cols
    g = jnp.concatenate([sums[i] for i in range(pieces)], axis=0) * scale
    inverse = lower_inverse(g[:, 0:n_all])
    old_coupling = g[:, n_all : 2 * n_all]

    drain(a1.at[pl.ds(0, n_row - 1)], 8)
    part = a1[0]
    for i in range(1, n_row):
        part = part + a1[i]
    a2[c] = part

    @pl.loop(0, n_col - 1)
    def _(i):
        rcopy(a2.at[c], a2.at[c], 9, (r, lax.rem(c + far_first(i, n_col), n_col))).start()

    new_basis[...] = dot_nn(inverse, basis[...])
    out_basis = pltpu.make_async_copy(new_basis, basis_o, loc.at[0])
    out_basis.start()
    new_image[...] = dot_nn(inverse, image[...])
    out_image = pltpu.make_async_copy(new_image, image_o, loc.at[1])
    out_image.start()
    base = dot_nt(dot_nn(inverse, old_coupling), inverse)
    last = jnp.swapaxes(inverse[:, n_all - 8 : n_all], 0, 1)
    last = jnp.where(lax.broadcasted_iota(jnp.int32, (8, n_all), 0) >= 8 - n_vec, last, 0.0)

    drain(a2.at[pl.ds(0, n_col - 1)], 9)
    part = a2[0]
    for i in range(1, n_col):
        part = part + a2[i]
    fresh = jnp.concatenate([jnp.zeros((4, n_all), F32), part[:, 0:n_all], part[:, 64 : 64 + n_all]], axis=0) * scale
    proj[...] = base + dot_nn(dot_nt(inverse, fresh), last)
    out_proj = pltpu.make_async_copy(proj, proj_o, loc.at[2])
    out_proj.start()
    out_proj.wait()
    out_basis.wait()
    out_image.wait()


def hand_out(a_in, b_in, c_in, a_out, b_out, c_out, sem):
    copies = [
        pltpu.make_async_copy(b_in, b_out, sem.at[0]),
        pltpu.make_async_copy(c_in, c_out, sem.at[1]),
        pltpu.make_async_copy(a_in, a_out, sem.at[2]),
    ]
    for copy in copies:
        copy.start()
    for copy in copies:
        copy.wait()


def local(tile_blocks, tile_rows, tile_cols, trial_vectors, basis_old, image_old):
    n_row = lax.axis_size("row")
    n_col = lax.axis_size("col")
    kt, ts, _ = tile_blocks.shape
    n_vec, width = trial_vectors.shape
    n_old = basis_old.shape[0]
    n_all = n_old + n_vec
    hbm = pl.BlockSpec(memory_space=pltpu.HBM)
    v = pltpu.VMEM
    operands = [
        pltpu.with_memory_space_constraint(x, pltpu.HBM)
        for x in (tile_rows, tile_cols, tile_blocks, trial_vectors, basis_old, image_old)
    ]
    outs = pl.pallas_call(
        functools.partial(kernel, n_row, n_col, float(width * n_row * n_col)),
        out_shape=(
            jax.ShapeDtypeStruct((n_all, n_all), F32),
            jax.ShapeDtypeStruct((n_all, width), F32),
            jax.ShapeDtypeStruct((n_all, width), F32),
        ),
        in_specs=[hbm] * 6,
        out_specs=(pl.BlockSpec(memory_space=pl.ANY),) * 3,
        scratch_shapes=[
            pltpu.SMEM((kt,), jnp.int32),
            pltpu.SMEM((kt,), jnp.int32),
            v((kt, ts, ts), BF16),
            v((n_vec, width), BF16),
            v((n_old, width), F32),
            v((n_old, width), F32),
            v((n_all, width), F32),
            v((n_all, width), F32),
            v((2 * n_all, width), F32),
            v((8 * n_row, n_vec, ts), BF16),
            v((8 * n_col, n_vec, ts), BF16),
            v((2, 128, ts), F32),
            v((128, ts), F32),
            v((2, 8, 128), jnp.int32),
            v((n_row // 8, 128, 512), BF16),
            v((n_col // 4, 128, 256), BF16),
            v((n_row // 2, 32, ts), F32),
            v((n_col, 32, ts), F32),
            v((n_row // 2 - 1, 32, ts), F32),
            v((n_col - 1, 32, ts), F32),
            v((n_all // 8, 8, 128), F32),
            v((n_row, 8, 128), F32),
            v((n_col, 8, 128), F32),
            v((n_all // 8, 8, 128), F32),
            v((n_row, 2, 128), F32),
            v((n_col, 2, 128), F32),
            v((n_all, width), F32),
            v((n_all, width), F32),
            v((n_all, n_all), F32),
            pltpu.SemaphoreType.DMA((6,)),
            pltpu.SemaphoreType.DMA((12, 2)),
            pltpu.SemaphoreType.DMA((n_row // 2,)),
        ],
        compiler_params=pltpu.CompilerParams(
            collective_id=0, has_side_effects=True, vmem_limit_bytes=32 << 20
        ),
    )(*operands)
    return pl.pallas_call(
        hand_out,
        out_shape=tuple(jax.ShapeDtypeStruct(o.shape, o.dtype) for o in outs),
        in_specs=[pl.BlockSpec(memory_space=pl.ANY)] * 3,
        out_specs=(hbm,) * 3,
        scratch_shapes=[pltpu.SemaphoreType.DMA((3,))],
        compiler_params=pltpu.CompilerParams(vmem_limit_bytes=32 << 20),
    )(*outs)


def solution(mesh):
    in_specs = (
        P(("row", "col"), None, None),
        P(("row", "col")),
        P(("row", "col")),
        P(None, ("col", "row")),
        P(None, ("col", "row")),
        P(None, ("col", "row")),
    )
    out_specs = (P(), P(None, ("col", "row")), P(None, ("col", "row")))
    return jax.shard_map(local, mesh=mesh, in_specs=in_specs, out_specs=out_specs, check_vma=False)
```

```python
import functools

import jax
import jax.numpy as jnp
from jax import lax
from jax.experimental import pallas as pl
from jax.experimental.pallas import tpu as pltpu
from jax.sharding import PartitionSpec as P

MESH = pl.DeviceIdType.MESH
F32 = jnp.float32
BF16 = jnp.bfloat16
HIGHEST = lax.Precision.HIGHEST


def dot_nt(a, b):
    return lax.dot_general(a, b, (((1,), (1,)), ((), ())), precision=HIGHEST, preferred_element_type=F32)


def dot_nn(a, b):
    return lax.dot_general(a, b, (((1,), (0,)), ((), ())), precision=HIGHEST, preferred_element_type=F32)


def lower_inverse(a, pause):
    n = a.shape[0]
    tiles = n // 8
    sub = lax.broadcasted_iota(jnp.int32, (8, n), 0)
    lane = lax.broadcasted_iota(jnp.int32, (8, n), 1)
    left = [a[8 * i : 8 * i + 8, :] for i in range(tiles)]
    right = [jnp.where(sub + 8 * i == lane, 1.0, 0.0).astype(F32) for i in range(tiles)]
    for j in range(n):
        if j == n * 3 // 4:
            pause()
        at, row = j // 8, j % 8
        pivot_left = left[at][row : row + 1, :]
        pivot_right = right[at][row : row + 1, :]
        inv = 1.0 / pivot_left[:, j : j + 1]
        pivot_left = pivot_left * inv
        pivot_right = pivot_right * inv
        for i in range(at, tiles):
            ratio = left[i][:, j : j + 1]
            if i == at:
                ratio = jnp.where(sub[:, :1] > row, ratio, 0.0)
            left[i] = left[i] - ratio * pivot_left
            right[i] = right[i] - ratio * pivot_right
    out = []
    for i in range(tiles):
        diag = jnp.sum(jnp.where(sub + 8 * i == lane, left[i], 0.0), axis=1, keepdims=True)
        out.append(right[i] / jnp.sqrt(diag))
    return jnp.concatenate(out, axis=0)


def kernel(
    n_row, n_col, total_cols,
    rows_h, cols_h, tiles_h, trial_h, basis_h, image_h,
    proj_o, basis_o, image_o,
    rows_s, cols_s, tiles, trial, old_basis, old_image, basis, image, mix,
    x_row, x_col, prod, prod2, keys, pick_row, pick_col, row_send, col_send, row_recv, col_recv,
    gram, e1, e2, sums, a1, a2, new_basis, new_image, proj,
    loc, sem, relay,
):
    r = lax.axis_index("row")
    c = lax.axis_index("col")
    n_old = basis_h.shape[0]
    n_vec = trial_h.shape[0]
    n_all = n_old + n_vec
    kt = tiles.shape[0]
    pieces = n_all // 8
    step = n_row // pieces
    piece = r // step
    owner = (r % step == 0) & (piece < pieces)

    local = [
        pltpu.make_async_copy(trial_h, trial, loc.at[0]),
        pltpu.make_async_copy(basis_h, old_basis, loc.at[1]),
        pltpu.make_async_copy(image_h, old_image, loc.at[2]),
        pltpu.make_async_copy(tiles_h, tiles, loc.at[3]),
        pltpu.make_async_copy(rows_h, rows_s, loc.at[4]),
        pltpu.make_async_copy(cols_h, cols_s, loc.at[5]),
    ]
    for copy in local:
        copy.start()

    bar = pltpu.get_barrier_semaphore()

    @pl.loop(1, n_row)
    def _(d):
        pl.semaphore_signal(bar, 1, device_id=(lax.rem(r + d, n_row), c), device_id_type=MESH)

    @pl.loop(1, n_col)
    def _(d):
        pl.semaphore_signal(bar, 1, device_id=(r, lax.rem(c + d, n_col)), device_id_type=MESH)

    local[0].wait()
    for j in range(8):
        block = trial[:, 128 * j : 128 * (j + 1)]
        x_row[r * 8 + j] = block
        x_col[c * 8 + j] = block
    pl.semaphore_wait(bar, n_row + n_col - 2)

    def rcopy(src, dst, k, dev):
        return pltpu.make_async_remote_copy(
            src, dst, sem.at[k, 0], sem.at[k, 1], device_id=dev, device_id_type=MESH
        )

    def drain(view, k):
        w = rcopy(view, view, k, (r, c))
        w.wait_send()
        w.wait_recv()

    def far_first(i, n):
        return lax.rem(n // 2 + (i + 1) // 2 * (1 - i % 2 * 2) + n, n)

    @pl.loop(0, n_col - 1)
    def _(i):
        own = pl.ds(c * 8, 8)
        rcopy(x_col.at[own], x_col.at[own], 1, (r, lax.rem(c // 8 + 1 - i % 2, 2) * 8 + lax.rem(c % 8 + far_first(i // 2, 8), 8))).start()

    half = n_row // 2
    pair = r // 2
    core = r % 2
    twin = (r + 1 - 2 * core, c)
    own = pl.ds(r * 8, 8)

    @pl.loop(0, half - 1)
    def _(i):
        d = far_first(i, half)
        to = lax.rem(pair + d, half) * 2 + core
        pltpu.make_async_remote_copy(
            x_row.at[own], x_row.at[own], sem.at[0, 0], relay.at[d], device_id=(to, c), device_id_type=MESH
        ).start()

    rcopy(x_row.at[own], x_row.at[own], 7, twin).start()

    local[4].wait()
    local[5].wait()

    def row_of(t):
        b = rows_s[t]
        return b // (8 * n_row) * 8 + b % 8

    def col_of(t):
        return cols_s[t] % (8 * n_row)

    lane = lax.broadcasted_iota(jnp.int32, (8, 128), 1)
    row_key = jnp.full((8, 128), -1, jnp.int32)
    col_key = jnp.full((8, 128), -1, jnp.int32)
    for t in range(kt):
        mine = lane // 4 == t
        row_key = jnp.where(mine, row_of(t) * 4 + lane % 4, row_key)
        col_key = jnp.where(mine, col_of(t) * 4 + lane % 4, col_key)
    keys[0] = col_key
    rcopy(keys.at[0], keys.at[1], 10, twin).start()

    local[1].wait()
    local[2].wait()
    basis[0:n_old, :] = old_basis[...]
    image[0:n_old, :] = old_image[...]
    basis[n_old:n_all, :] = trial[...].astype(F32)
    image[n_old:n_all, :] = jnp.zeros((n_vec, image.shape[1]), F32)
    mix[0:n_all, :] = basis[...]
    mix[n_all : 2 * n_all, :] = image[...]
    g = dot_nt(basis[...], mix[...])
    gram[...] = jnp.zeros(gram.shape, F32)
    for i in range(n_all // 8):
        gram[i, :, 0 : 2 * n_all] = g[8 * i : 8 * i + 8, :]

    @pl.loop(0, pieces)
    def _(p):
        @pl.when(p * step != r)
        def _():
            rcopy(gram.at[p], e1.at[r], 2, (p * step, c)).start()

    drain(keys.at[1], 10)
    key = jnp.concatenate([jnp.concatenate([keys[0]] * 2 + [keys[1]] * 2, axis=1)] * 16, axis=0)
    at = lax.broadcasted_iota(jnp.int32, (128, 512), 0)
    at = (at // 32 * 2 + core) * 32 + at % 32

    @pl.loop(0, half // 4)
    def _(s):
        pick_row[s] = jnp.where(at + s * 256 == key, 1.0, 0.0).astype(BF16)

    key2 = jnp.concatenate([jnp.concatenate([row_key] * 2, axis=1)] * 16, axis=0)
    at2 = lax.broadcasted_iota(jnp.int32, (128, 256), 0)

    @pl.loop(0, n_col // 4)
    def _(s):
        pick_col[s] = jnp.where(at2 + s * 128 == key2, 1.0, 0.0).astype(BF16)

    local[3].wait()
    prod[...] = jnp.zeros(prod.shape, F32)

    def products(which, x, index, along):
        if True:
            out = []
            for t in range(kt):
                out.append(
                    lax.dot_general(
                        x[index(t)], tiles[t], (((1,), (along,)), ((), ())), preferred_element_type=F32)
                )
            prod[which, 0 : 4 * kt, :] = jnp.concatenate(out, axis=0)

    def split(p):
        high = p.astype(BF16)
        return high, (p - high.astype(F32)).astype(BF16)

    drain(x_col.at[pl.ds(0, (n_col - 1) * 8)], 1)
    products(1, x_col, row_of, 0)
    rcopy(prod.at[1], prod2, 11, twin).start()

    @pl.when(owner)
    def _():
        rcopy(e1.at[pl.ds(0, n_row - 1)], e1.at[pl.ds(0, n_row - 1)], 2, (r, c)).wait_recv()
        gone = gram.at[pl.ds(0, pieces - 1)]
        rcopy(gone, gone, 2, (r, c)).wait_send()
        e1[r] = gram[piece]
        part = e1[0]
        for i in range(1, n_row):
            part = part + e1[i]
        e2[c] = part

        @pl.loop(0, n_col - 1)
        def _(i):
            rcopy(e2.at[c], e2.at[c], 5, (r, lax.rem(c + far_first(i, n_col), n_col))).start()

    @pl.when(jnp.logical_not(owner))
    def _():
        rcopy(gram, gram, 2, (r, c)).wait_send()

    @pl.loop(0, half - 1)
    def _(i):
        d = far_first(half - 2 - i, half)
        at = pl.ds(lax.rem(pair - d + half, half) * 16 + core * 8, 8)
        piece_in = x_row.at[at]
        pltpu.make_async_remote_copy(
            piece_in, piece_in, sem.at[0, 0], relay.at[d], device_id=(r, c), device_id_type=MESH
        ).wait_recv()
        rcopy(piece_in, piece_in, 7, twin).start()

    drain(prod2, 11)
    both = jnp.concatenate([*split(prod[1]), *split(prod2[...])], axis=0)

    for s in range(half // 4):
        placed = lax.dot_general(pick_row[s], both, (((1,), (0,)), ((), ())), preferred_element_type=F32)
        row_send[4 * s : 4 * s + 4] = placed.reshape(4, 32, 128)

    @pl.loop(0, half - 1)
    def _(i):
        d = far_first(i, half)
        to = lax.rem(pair + d, half)
        rcopy(row_send.at[to], row_recv.at[d - 1], 3, (to * 2 + core, c)).start()

    drain(x_row.at[pl.ds(0, half * 8)], 7)
    sent = x_row.at[pl.ds(0, (half - 1) * 8)]
    rcopy(sent, sent, 0, (r, c)).wait_send()
    products(0, x_row, col_of, 1)
    both = jnp.concatenate(split(prod[0]), axis=0)

    for s in range(n_col // 4):
        placed = lax.dot_general(pick_col[s], both, (((1,), (0,)), ((), ())), preferred_element_type=F32)
        col_send[4 * s : 4 * s + 4] = placed.reshape(4, 32, 128)

    @pl.loop(0, n_col - 1)
    def _(i):
        d = far_first(i, n_col)
        to = lax.rem(c + d, n_col)
        rcopy(col_send.at[to], col_recv.at[d - 1], 4, (r, to)).start()

    @pl.when(owner)
    def _():
        drain(e2.at[pl.ds(0, n_col - 1)], 5)
        part = e2[0]
        for i in range(1, n_col):
            part = part + e2[i]
        sums[piece] = part

        @pl.loop(0, n_row - 1)
        def _(i):
            to = lax.rem(r + far_first(i, n_row), n_row)
            rcopy(sums.at[piece], sums.at[piece], 6, (to, c)).start()

    drain(row_recv, 3)
    drain(col_recv, 4)
    acc = row_send[pair] + col_send[c]
    for i in range(half - 1):
        acc = acc + row_recv[i]
    for i in range(n_col - 1):
        acc = acc + col_recv[i]
    for j in range(8):
        image[n_old:n_all, 128 * j : 128 * (j + 1)] = acc[n_vec * j : n_vec * (j + 1), :]
    fresh = image[n_all - 8 : n_all, :]
    fresh = dot_nt(fresh, basis[...])
    a1[r] = jnp.zeros((2, 128), F32)
    a1[r, :, 0:n_all] = fresh[4:6, :]
    a1[r, :, 64 : 64 + n_all] = fresh[6:8, :]

    @pl.loop(0, n_row - 1)
    def _(i):
        rcopy(a1.at[r], a1.at[r], 8, (lax.rem(r + far_first(i, n_row), n_row), c)).start()

    @pl.when(owner)
    def _():
        came = sums.at[pl.ds(0, pieces - 1)]
        rcopy(came, came, 6, (r, c)).wait_recv()
        gone = e1.at[pl.ds(0, n_row - 1)]
        rcopy(gone, gone, 6, (r, c)).wait_send()

    @pl.when(jnp.logical_not(owner))
    def _():
        rcopy(sums, sums, 6, (r, c)).wait_recv()

    scale = 1.0 / total_cols
    g = jnp.concatenate([sums[i] for i in range(pieces)], axis=0) * scale
    def pass_on():

        drain(a1.at[pl.ds(0, n_row - 1)], 8)
        part = a1[0]
        for i in range(1, n_row):
            part = part + a1[i]
        a2[c] = part

        @pl.loop(0, n_col - 1)
        def _(i):
            rcopy(a2.at[c], a2.at[c], 9, (r, lax.rem(c // 8 + 1 - i % 2, 2) * 8 + lax.rem(c % 8 + far_first(i // 2, 8), 8))).start()

    inverse = lower_inverse(g[:, 0:n_all], pass_on)
    old_coupling = g[:, n_all : 2 * n_all]
    new_basis[...] = dot_nn(inverse, basis[...])
    out_basis = pltpu.make_async_copy(new_basis, basis_o, loc.at[0])
    out_basis.start()
    new_image[...] = dot_nn(inverse, image[...])
    out_image = pltpu.make_async_copy(new_image, image_o, loc.at[1])
    out_image.start()
    base = dot_nt(dot_nn(inverse, old_coupling), inverse)
    last = jnp.swapaxes(inverse[:, n_all - 8 : n_all], 0, 1)
    last = jnp.where(lax.broadcasted_iota(jnp.int32, (8, n_all), 0) >= 8 - n_vec, last, 0.0)

    drain(a2.at[pl.ds(0, n_col - 1)], 9)
    part = a2[0]
    for i in range(1, n_col):
        part = part + a2[i]
    fresh = jnp.concatenate([jnp.zeros((4, n_all), F32), part[:, 0:n_all], part[:, 64 : 64 + n_all]], axis=0) * scale
    proj[...] = base + dot_nn(dot_nt(inverse, fresh), last)
    out_proj = pltpu.make_async_copy(proj, proj_o, loc.at[2])
    out_proj.start()
    out_proj.wait()
    out_basis.wait()
    out_image.wait()


def hand_out(a_in, b_in, c_in, a_out, b_out, c_out, sem):
    copies = [
        pltpu.make_async_copy(b_in, b_out, sem.at[0]),
        pltpu.make_async_copy(c_in, c_out, sem.at[1]),
        pltpu.make_async_copy(a_in, a_out, sem.at[2]),
    ]
    for copy in copies:
        copy.start()
    for copy in copies:
        copy.wait()


def local(tile_blocks, tile_rows, tile_cols, trial_vectors, basis_old, image_old):
    n_row = lax.axis_size("row")
    n_col = lax.axis_size("col")
    kt, ts, _ = tile_blocks.shape
    n_vec, width = trial_vectors.shape
    n_old = basis_old.shape[0]
    n_all = n_old + n_vec
    hbm = pl.BlockSpec(memory_space=pltpu.HBM)
    v = pltpu.VMEM
    operands = [
        pltpu.with_memory_space_constraint(x, pltpu.HBM)
        for x in (tile_rows, tile_cols, tile_blocks, trial_vectors, basis_old, image_old)
    ]
    outs = pl.pallas_call(
        functools.partial(kernel, n_row, n_col, float(width * n_row * n_col)),
        out_shape=(
            jax.ShapeDtypeStruct((n_all, n_all), F32),
            jax.ShapeDtypeStruct((n_all, width), F32),
            jax.ShapeDtypeStruct((n_all, width), F32),
        ),
        in_specs=[hbm] * 6,
        out_specs=(pl.BlockSpec(memory_space=pl.ANY),) * 3,
        scratch_shapes=[
            pltpu.SMEM((kt,), jnp.int32),
            pltpu.SMEM((kt,), jnp.int32),
            v((kt, ts, ts), BF16),
            v((n_vec, width), BF16),
            v((n_old, width), F32),
            v((n_old, width), F32),
            v((n_all, width), F32),
            v((n_all, width), F32),
            v((2 * n_all, width), F32),
            v((8 * n_row, n_vec, ts), BF16),
            v((8 * n_col, n_vec, ts), BF16),
            v((2, 128, ts), F32),
            v((128, ts), F32),
            v((2, 8, 128), jnp.int32),
            v((n_row // 8, 128, 512), BF16),
            v((n_col // 4, 128, 256), BF16),
            v((n_row // 2, 32, ts), F32),
            v((n_col, 32, ts), F32),
            v((n_row // 2 - 1, 32, ts), F32),
            v((n_col - 1, 32, ts), F32),
            v((n_all // 8, 8, 128), F32),
            v((n_row, 8, 128), F32),
            v((n_col, 8, 128), F32),
            v((n_all // 8, 8, 128), F32),
            v((n_row, 2, 128), F32),
            v((n_col, 2, 128), F32),
            v((n_all, width), F32),
            v((n_all, width), F32),
            v((n_all, n_all), F32),
            pltpu.SemaphoreType.DMA((6,)),
            pltpu.SemaphoreType.DMA((12, 2)),
            pltpu.SemaphoreType.DMA((n_row // 2,)),
        ],
        compiler_params=pltpu.CompilerParams(
            collective_id=0, has_side_effects=True, vmem_limit_bytes=32 << 20
        ),
    )(*operands)
    return pl.pallas_call(
        hand_out,
        out_shape=tuple(jax.ShapeDtypeStruct(o.shape, o.dtype) for o in outs),
        in_specs=[pl.BlockSpec(memory_space=pl.ANY)] * 3,
        out_specs=(hbm,) * 3,
        scratch_shapes=[pltpu.SemaphoreType.DMA((3,))],
        compiler_params=pltpu.CompilerParams(vmem_limit_bytes=32 << 20),
    )(*outs)


def solution(mesh):
    in_specs = (
        P(("row", "col"), None, None),
        P(("row", "col")),
        P(("row", "col")),
        P(None, ("col", "row")),
        P(None, ("col", "row")),
        P(None, ("col", "row")),
    )
    out_specs = (P(), P(None, ("col", "row")), P(None, ("col", "row")))
    return jax.shard_map(local, mesh=mesh, in_specs=in_specs, out_specs=out_specs, check_vma=False)
```

```python
import functools

import jax
import jax.numpy as jnp
from jax import lax
from jax.experimental import pallas as pl
from jax.experimental.pallas import tpu as pltpu
from jax.sharding import PartitionSpec as P

MESH = pl.DeviceIdType.MESH
F32 = jnp.float32
BF16 = jnp.bfloat16
HIGHEST = lax.Precision.HIGHEST


def dot_nt(a, b):
    return lax.dot_general(a, b, (((1,), (1,)), ((), ())), precision=HIGHEST, preferred_element_type=F32)


def dot_nn(a, b):
    return lax.dot_general(a, b, (((1,), (0,)), ((), ())), precision=HIGHEST, preferred_element_type=F32)


def lower_inverse(a, pause):
    n = a.shape[0]
    tiles = n // 8
    sub = lax.broadcasted_iota(jnp.int32, (8, n), 0)
    lane = lax.broadcasted_iota(jnp.int32, (8, n), 1)
    left = [a[8 * i : 8 * i + 8, :] for i in range(tiles)]
    right = [jnp.where(sub + 8 * i == lane, 1.0, 0.0).astype(F32) for i in range(tiles)]
    for j in range(n):
        if j == n * 7 // 8:
            pause()
        at, row = j // 8, j % 8
        pivot_left = left[at][row : row + 1, :]
        pivot_right = right[at][row : row + 1, :]
        inv = 1.0 / pivot_left[:, j : j + 1]
        pivot_left = pivot_left * inv
        pivot_right = pivot_right * inv
        for i in range(at, tiles):
            ratio = left[i][:, j : j + 1]
            if i == at:
                ratio = jnp.where(sub[:, :1] > row, ratio, 0.0)
            left[i] = left[i] - ratio * pivot_left
            right[i] = right[i] - ratio * pivot_right
    out = []
    for i in range(tiles):
        diag = jnp.sum(jnp.where(sub + 8 * i == lane, left[i], 0.0), axis=1, keepdims=True)
        out.append(right[i] / jnp.sqrt(diag))
    return jnp.concatenate(out, axis=0)


def kernel(
    n_row, n_col, total_cols,
    rows_h, cols_h, tiles_h, trial_h, basis_h, image_h,
    proj_o, basis_o, image_o,
    rows_s, cols_s, tiles, trial, old_basis, old_image, basis, image, mix,
    x_row, x_col, prod, prod2, keys, pick_row, pick_col, row_send, col_send, row_recv, col_recv,
    gram, e1, e2, sums, a1, a2, new_basis, new_image, proj,
    loc, sem, relay,
):
    r = lax.axis_index("row")
    c = lax.axis_index("col")
    n_old = basis_h.shape[0]
    n_vec = trial_h.shape[0]
    n_all = n_old + n_vec
    kt = tiles.shape[0]
    pieces = n_all // 8
    step = n_row // pieces
    piece = r // step
    owner = (r % step == 0) & (piece < pieces)

    local = [
        pltpu.make_async_copy(trial_h, trial, loc.at[0]),
        pltpu.make_async_copy(basis_h, old_basis, loc.at[1]),
        pltpu.make_async_copy(image_h, old_image, loc.at[2]),
        pltpu.make_async_copy(tiles_h, tiles, loc.at[3]),
        pltpu.make_async_copy(rows_h, rows_s, loc.at[4]),
        pltpu.make_async_copy(cols_h, cols_s, loc.at[5]),
    ]
    for copy in local:
        copy.start()

    bar = pltpu.get_barrier_semaphore()

    @pl.loop(1, n_row)
    def _(d):
        pl.semaphore_signal(bar, 1, device_id=(lax.rem(r + d, n_row), c), device_id_type=MESH)

    @pl.loop(1, n_col)
    def _(d):
        pl.semaphore_signal(bar, 1, device_id=(r, lax.rem(c + d, n_col)), device_id_type=MESH)

    local[0].wait()
    for j in range(8):
        block = trial[:, 128 * j : 128 * (j + 1)]
        x_row[r * 8 + j] = block
        x_col[c * 8 + j] = block
    pl.semaphore_wait(bar, n_row + n_col - 2)

    def rcopy(src, dst, k, dev):
        return pltpu.make_async_remote_copy(
            src, dst, sem.at[k, 0], sem.at[k, 1], device_id=dev, device_id_type=MESH
        )

    def drain(view, k):
        w = rcopy(view, view, k, (r, c))
        w.wait_send()
        w.wait_recv()

    def far_first(i, n):
        return lax.rem(n // 2 + (i + 1) // 2 * (1 - i % 2 * 2) + n, n)

    @pl.loop(0, n_col - 1)
    def _(i):
        own = pl.ds(c * 8, 8)
        rcopy(x_col.at[own], x_col.at[own], 1, (r, lax.rem(c // 8 + 1 - i % 2, 2) * 8 + lax.rem(c % 8 + far_first(i // 2, 8), 8))).start()

    half = n_row // 2
    pair = r // 2
    core = r % 2
    twin = (r + 1 - 2 * core, c)
    own = pl.ds(r * 8, 8)

    @pl.loop(0, half - 1)
    def _(i):
        d = far_first(i, half)
        to = lax.rem(pair + d, half) * 2 + core
        pltpu.make_async_remote_copy(
            x_row.at[own], x_row.at[own], sem.at[0, 0], relay.at[d], device_id=(to, c), device_id_type=MESH
        ).start()

    rcopy(x_row.at[own], x_row.at[own], 7, twin).start()

    local[4].wait()
    local[5].wait()

    def row_of(t):
        b = rows_s[t]
        return b // (8 * n_row) * 8 + b % 8

    def col_of(t):
        return cols_s[t] % (8 * n_row)

    lane = lax.broadcasted_iota(jnp.int32, (8, 128), 1)
    row_key = jnp.full((8, 128), -1, jnp.int32)
    col_key = jnp.full((8, 128), -1, jnp.int32)
    for t in range(kt):
        mine = lane // 4 == t
        row_key = jnp.where(mine, row_of(t) * 4 + lane % 4, row_key)
        col_key = jnp.where(mine, col_of(t) * 4 + lane % 4, col_key)
    keys[0] = col_key
    rcopy(keys.at[0], keys.at[1], 10, twin).start()

    local[1].wait()
    local[2].wait()
    basis[0:n_old, :] = old_basis[...]
    image[0:n_old, :] = old_image[...]
    basis[n_old:n_all, :] = trial[...].astype(F32)
    image[n_old:n_all, :] = jnp.zeros((n_vec, image.shape[1]), F32)
    mix[0:n_all, :] = basis[...]
    mix[n_all : 2 * n_all, :] = image[...]
    g = dot_nt(basis[...], mix[...])
    gram[...] = jnp.zeros(gram.shape, F32)
    for i in range(n_all // 8):
        gram[i, :, 0 : 2 * n_all] = g[8 * i : 8 * i + 8, :]

    @pl.loop(0, pieces)
    def _(p):
        @pl.when(p * step != r)
        def _():
            rcopy(gram.at[p], e1.at[r], 2, (p * step, c)).start()

    drain(keys.at[1], 10)
    key = jnp.concatenate([jnp.concatenate([keys[0]] * 2 + [keys[1]] * 2, axis=1)] * 16, axis=0)
    at = lax.broadcasted_iota(jnp.int32, (128, 512), 0)
    at = (at // 32 * 2 + core) * 32 + at % 32

    @pl.loop(0, half // 4)
    def _(s):
        pick_row[s] = jnp.where(at + s * 256 == key, 1.0, 0.0).astype(BF16)

    key2 = jnp.concatenate([jnp.concatenate([row_key] * 2, axis=1)] * 16, axis=0)
    at2 = lax.broadcasted_iota(jnp.int32, (128, 256), 0)

    @pl.loop(0, n_col // 4)
    def _(s):
        pick_col[s] = jnp.where(at2 + s * 128 == key2, 1.0, 0.0).astype(BF16)

    local[3].wait()
    prod[...] = jnp.zeros(prod.shape, F32)

    def products(which, x, index, along):
        if True:
            out = []
            for t in range(kt):
                out.append(
                    lax.dot_general(
                        x[index(t)], tiles[t], (((1,), (along,)), ((), ())), preferred_element_type=F32)
                )
            prod[which, 0 : 4 * kt, :] = jnp.concatenate(out, axis=0)

    def split(p):
        high = p.astype(BF16)
        return high, (p - high.astype(F32)).astype(BF16)

    drain(x_col.at[pl.ds(0, (n_col - 1) * 8)], 1)
    products(1, x_col, row_of, 0)
    rcopy(prod.at[1], prod2, 11, twin).start()

    @pl.when(owner)
    def _():
        rcopy(e1.at[pl.ds(0, n_row - 1)], e1.at[pl.ds(0, n_row - 1)], 2, (r, c)).wait_recv()
        gone = gram.at[pl.ds(0, pieces - 1)]
        rcopy(gone, gone, 2, (r, c)).wait_send()
        e1[r] = gram[piece]
        part = e1[0]
        for i in range(1, n_row):
            part = part + e1[i]
        e2[c] = part

        @pl.loop(0, n_col - 1)
        def _(i):
            rcopy(e2.at[c], e2.at[c], 5, (r, lax.rem(c + far_first(i, n_col), n_col))).start()

    @pl.when(jnp.logical_not(owner))
    def _():
        rcopy(gram, gram, 2, (r, c)).wait_send()

    @pl.loop(0, half - 1)
    def _(i):
        d = far_first(half - 2 - i, half)
        at = pl.ds(lax.rem(pair - d + half, half) * 16 + core * 8, 8)
        piece_in = x_row.at[at]
        pltpu.make_async_remote_copy(
            piece_in, piece_in, sem.at[0, 0], relay.at[d], device_id=(r, c), device_id_type=MESH
        ).wait_recv()
        rcopy(piece_in, piece_in, 7, twin).start()

    drain(prod2, 11)
    both = jnp.concatenate([*split(prod[1]), *split(prod2[...])], axis=0)

    for s in range(half // 4):
        placed = lax.dot_general(pick_row[s], both, (((1,), (0,)), ((), ())), preferred_element_type=F32)
        row_send[4 * s : 4 * s + 4] = placed.reshape(4, 32, 128)

    @pl.loop(0, half - 1)
    def _(i):
        d = far_first(i, half)
        to = lax.rem(pair + d, half)
        rcopy(row_send.at[to], row_recv.at[d - 1], 3, (to * 2 + core, c)).start()

    drain(x_row.at[pl.ds(0, half * 8)], 7)
    sent = x_row.at[pl.ds(0, (half - 1) * 8)]
    rcopy(sent, sent, 0, (r, c)).wait_send()
    products(0, x_row, col_of, 1)
    both = jnp.concatenate(split(prod[0]), axis=0)

    for s in range(n_col // 4):
        placed = lax.dot_general(pick_col[s], both, (((1,), (0,)), ((), ())), preferred_element_type=F32)
        col_send[4 * s : 4 * s + 4] = placed.reshape(4, 32, 128)

    @pl.loop(0, n_col - 1)
    def _(i):
        d = far_first(i, n_col)
        to = lax.rem(c + d, n_col)
        rcopy(col_send.at[to], col_recv.at[d - 1], 4, (r, to)).start()

    @pl.when(owner)
    def _():
        drain(e2.at[pl.ds(0, n_col - 1)], 5)
        part = e2[0]
        for i in range(1, n_col):
            part = part + e2[i]
        sums[piece] = part

        @pl.loop(0, n_row - 1)
        def _(i):
            to = lax.rem(r + far_first(i, n_row), n_row)
            rcopy(sums.at[piece], sums.at[piece], 6, (to, c)).start()

    drain(row_recv, 3)
    drain(col_recv, 4)
    acc = row_send[pair] + col_send[c]
    for i in range(half - 1):
        acc = acc + row_recv[i]
    for i in range(n_col - 1):
        acc = acc + col_recv[i]
    for j in range(8):
        image[n_old:n_all, 128 * j : 128 * (j + 1)] = acc[n_vec * j : n_vec * (j + 1), :]
    fresh = image[n_all - 8 : n_all, :]
    fresh = dot_nt(fresh, basis[...])
    a1[r] = jnp.zeros((2, 128), F32)
    a1[r, :, 0:n_all] = fresh[4:6, :]
    a1[r, :, 64 : 64 + n_all] = fresh[6:8, :]

    @pl.loop(0, n_row - 1)
    def _(i):
        rcopy(a1.at[r], a1.at[r], 8, (lax.rem(r + far_first(i, n_row), n_row), c)).start()

    @pl.when(owner)
    def _():
        came = sums.at[pl.ds(0, pieces - 1)]
        rcopy(came, came, 6, (r, c)).wait_recv()
        gone = e1.at[pl.ds(0, n_row - 1)]
        rcopy(gone, gone, 6, (r, c)).wait_send()

    @pl.when(jnp.logical_not(owner))
    def _():
        rcopy(sums, sums, 6, (r, c)).wait_recv()

    scale = 1.0 / total_cols
    g = jnp.concatenate([sums[i] for i in range(pieces)], axis=0) * scale
    def pass_on():

        drain(a1.at[pl.ds(0, n_row - 1)], 8)
        part = a1[0]
        for i in range(1, n_row):
            part = part + a1[i]
        a2[c] = part

        @pl.loop(0, n_col - 1)
        def _(i):
            rcopy(a2.at[c], a2.at[c], 9, (r, lax.rem(c // 8 + 1 - i % 2, 2) * 8 + lax.rem(c % 8 + far_first(i // 2, 8), 8))).start()

    inverse = lower_inverse(g[:, 0:n_all], pass_on)
    old_coupling = g[:, n_all : 2 * n_all]
    new_basis[...] = dot_nn(inverse, basis[...])
    out_basis = pltpu.make_async_copy(new_basis, basis_o, loc.at[0])
    out_basis.start()
    new_image[...] = dot_nn(inverse, image[...])
    out_image = pltpu.make_async_copy(new_image, image_o, loc.at[1])
    out_image.start()
    base = dot_nt(dot_nn(inverse, old_coupling), inverse)
    last = jnp.swapaxes(inverse[:, n_all - 8 : n_all], 0, 1)
    last = jnp.where(lax.broadcasted_iota(jnp.int32, (8, n_all), 0) >= 8 - n_vec, last, 0.0)

    drain(a2.at[pl.ds(0, n_col - 1)], 9)
    part = a2[0]
    for i in range(1, n_col):
        part = part + a2[i]
    fresh = jnp.concatenate([jnp.zeros((4, n_all), F32), part[:, 0:n_all], part[:, 64 : 64 + n_all]], axis=0) * scale
    proj[...] = base + dot_nn(dot_nt(inverse, fresh), last)
    out_proj = pltpu.make_async_copy(proj, proj_o, loc.at[2])
    out_proj.start()
    out_proj.wait()
    out_basis.wait()
    out_image.wait()


def hand_out(a_in, b_in, c_in, a_out, b_out, c_out, sem):
    copies = [
        pltpu.make_async_copy(b_in, b_out, sem.at[0]),
        pltpu.make_async_copy(c_in, c_out, sem.at[1]),
        pltpu.make_async_copy(a_in, a_out, sem.at[2]),
    ]
    for copy in copies:
        copy.start()
    for copy in copies:
        copy.wait()


def local(tile_blocks, tile_rows, tile_cols, trial_vectors, basis_old, image_old):
    n_row = lax.axis_size("row")
    n_col = lax.axis_size("col")
    kt, ts, _ = tile_blocks.shape
    n_vec, width = trial_vectors.shape
    n_old = basis_old.shape[0]
    n_all = n_old + n_vec
    hbm = pl.BlockSpec(memory_space=pltpu.HBM)
    v = pltpu.VMEM
    operands = [
        pltpu.with_memory_space_constraint(x, pltpu.HBM)
        for x in (tile_rows, tile_cols, tile_blocks, trial_vectors, basis_old, image_old)
    ]
    outs = pl.pallas_call(
        functools.partial(kernel, n_row, n_col, float(width * n_row * n_col)),
        out_shape=(
            jax.ShapeDtypeStruct((n_all, n_all), F32),
            jax.ShapeDtypeStruct((n_all, width), F32),
            jax.ShapeDtypeStruct((n_all, width), F32),
        ),
        in_specs=[hbm] * 6,
        out_specs=(pl.BlockSpec(memory_space=pl.ANY),) * 3,
        scratch_shapes=[
            pltpu.SMEM((kt,), jnp.int32),
            pltpu.SMEM((kt,), jnp.int32),
            v((kt, ts, ts), BF16),
            v((n_vec, width), BF16),
            v((n_old, width), F32),
            v((n_old, width), F32),
            v((n_all, width), F32),
            v((n_all, width), F32),
            v((2 * n_all, width), F32),
            v((8 * n_row, n_vec, ts), BF16),
            v((8 * n_col, n_vec, ts), BF16),
            v((2, 128, ts), F32),
            v((128, ts), F32),
            v((2, 8, 128), jnp.int32),
            v((n_row // 8, 128, 512), BF16),
            v((n_col // 4, 128, 256), BF16),
            v((n_row // 2, 32, ts), F32),
            v((n_col, 32, ts), F32),
            v((n_row // 2 - 1, 32, ts), F32),
            v((n_col - 1, 32, ts), F32),
            v((n_all // 8, 8, 128), F32),
            v((n_row, 8, 128), F32),
            v((n_col, 8, 128), F32),
            v((n_all // 8, 8, 128), F32),
            v((n_row, 2, 128), F32),
            v((n_col, 2, 128), F32),
            v((n_all, width), F32),
            v((n_all, width), F32),
            v((n_all, n_all), F32),
            pltpu.SemaphoreType.DMA((6,)),
            pltpu.SemaphoreType.DMA((12, 2)),
            pltpu.SemaphoreType.DMA((n_row // 2,)),
        ],
        compiler_params=pltpu.CompilerParams(
            collective_id=0, has_side_effects=True, vmem_limit_bytes=32 << 20
        ),
    )(*operands)
    return pl.pallas_call(
        hand_out,
        out_shape=tuple(jax.ShapeDtypeStruct(o.shape, o.dtype) for o in outs),
        in_specs=[pl.BlockSpec(memory_space=pl.ANY)] * 3,
        out_specs=(hbm,) * 3,
        scratch_shapes=[pltpu.SemaphoreType.DMA((3,))],
        compiler_params=pltpu.CompilerParams(vmem_limit_bytes=32 << 20),
    )(*outs)


def solution(mesh):
    in_specs = (
        P(("row", "col"), None, None),
        P(("row", "col")),
        P(("row", "col")),
        P(None, ("col", "row")),
        P(None, ("col", "row")),
        P(None, ("col", "row")),
    )
    out_specs = (P(), P(None, ("col", "row")), P(None, ("col", "row")))
    return jax.shard_map(local, mesh=mesh, in_specs=in_specs, out_specs=out_specs, check_vma=False)
```
